32 devices in a mesh: slab: 2 (over x), tile: 16 (over z, y, core).
Axes of the slice: x: 2, y: 2, z: 4, core: 2. Of those that a mesh axis runs over, the one named last changes fastest.
Arguments:
- ensemble: bfloat16 [512, 131072], P('tile', 'slab'), parts along dimension 1, may hold values from -6 to 6
- predicted: bfloat16 [512, 8192], P('tile', 'slab'), parts along dimension 1, may hold values from -6 to 6
- perturb: bfloat16 [512, 8192], P('tile', 'slab'), parts along dimension 1, may hold values from -5 to 5
- observed: float32 [8192], P('slab'), parts along dimension 0, may hold values from -6 to 6
- noise_scale: float32 [8192], P('slab'), parts along dimension 0, may hold values from 0.5 to 2
- block_list: int32 [16, 8], replicated, may hold values from 0 to 31, as said below
- block_count: int32 [16], replicated, may hold values from 1 to 8, as said below
- taper_class: int32 [16, 8], replicated, may hold values from 0 to 7
- taper_table: float32 [8], replicated, may hold values from 0.1 to 1
Outputs:
- updated: bfloat16 [512, 131072], P('tile', 'slab'), parts along dimension 1
The draws below stay inside these ranges and needn't reach their ends.
There are 2 independent parts, one for each index of `slab`. The reference program is written for one: setup_inputs(seed, part) draws one part's arguments, and reference() takes and returns one part's arrays. A program takes and returns all parts, laid end to end along the dimension named above; an argument that names none is the same for every part. Nothing has to cross between parts.
Inputs may be any that keep to these rules, and one draw needn't show every extreme that they name: `block_list`: every entry of row t names a block b with max(0, t - 2) <= b // 2 <= min(15, t + 2); entries may repeat. `block_count`: some tile uses all slots.
All inputs are finite; a program needn't handle non-finite values.
Results may differ from the reference program's by a relative error of at most 0.0047.
Values may be sent and summed in bfloat16 or wider, within the bound.
A program may use at most 64 MiB of HBM per device.

```python
import math
import jax
import jax.numpy as jnp
from jax import lax

MEMBERS = 512
CB = 128
KMAX = 8
REACH = 2
NBD = 2
NCLASS = 8
CT = 4096
NTILES = 16
NCELL = 65536
NBLK = 32
NDATA = 4096


def draw_block_list(key, part):
    key_off = jax.random.fold_in(key, 11)
    key_which = jax.random.fold_in(key, 12)
    tiles = jnp.arange(NTILES, dtype=jnp.int32)[:, None]
    offset = jax.random.randint(key_off, (NTILES, KMAX), -REACH, REACH + 1, dtype=jnp.int32)
    owner = jnp.clip(tiles + offset, 0, NTILES - 1)
    which = jax.random.randint(key_which, (NTILES, KMAX), 0, NBD, dtype=jnp.int32)
    ids = owner * NBD + which
    ids = ids.at[0, 0].set(0)
    ids = ids.at[NTILES - 1, 0].set(NTILES * NBD - 1)
    return ids.astype(jnp.int32)


def draw_block_count(key, part):
    key_count = jax.random.fold_in(key, 21)
    key_pos = jax.random.fold_in(key, 22)
    counts = jax.random.randint(key_count, (NTILES,), 1, KMAX + 1, dtype=jnp.int32)
    position = jax.random.randint(key_pos, (), 0, NTILES, dtype=jnp.int32)
    full = jnp.arange(NTILES, dtype=jnp.int32) == position
    return jnp.where(full, KMAX, counts).astype(jnp.int32)


def set_ends(result, rng, low, high):
    longest = result.shape.index(max(result.shape))
    spots = []
    for shift in (0, 1):
        where = [jax.random.randint(jax.random.fold_in(rng, axis), (), 0, length) for axis, length in enumerate(result.shape)]
        where[longest] = (where[longest] + shift) % result.shape[longest]
        spots.append(tuple(where))
    return result.at[spots[0]].set(low).at[spots[1]].set(high)


def shard_levels(own_key, shape, split, least, top_value):
    def one(dim, parts):
        draws = jax.random.uniform(jax.random.fold_in(jax.random.fold_in(own_key, 6), dim), (parts,), jnp.float32, least / len(split), top_value / len(split))
        return jnp.repeat(jnp.exp(draws), shape[dim] // parts).reshape((-1,) + (1,) * (len(shape) - dim - 1))

    level = one(*split[0])
    for cut in split[1:]:
        level = level * one(*cut)
    return level


def gaussian(rng, shape, spread, reach, split=(), held_as=jnp.bfloat16):
    level = shard_levels(rng, shape, split, -0.22, 0.18) if split else 1.0
    entries = jax.random.normal(rng, shape, jnp.float32) * spread * level
    return jnp.minimum(jnp.maximum(entries, -reach), reach).astype(held_as)


def setup_inputs(seed: int = 0, part: int = 0) -> dict:
    key_list = jax.random.split(jax.random.key(seed), 10)
    own_keys = jax.random.split(jax.random.fold_in(key_list[9], part), 10)
    ensemble = gaussian(own_keys[0], (MEMBERS, NCELL), 1.0, 6.0, ((0, 16),))
    predicted = gaussian(own_keys[1], (MEMBERS, NDATA), 1.0, 6.0, ((0, 16),))
    perturb = gaussian(own_keys[2], (MEMBERS, NDATA), 1.0, 5.0, ((0, 16),))
    observed = gaussian(own_keys[3], (NDATA,), 1.0, 6.0, (), jnp.float32)
    noise_scale = jnp.clip(jnp.exp(jax.random.uniform(own_keys[4], (NDATA,), jnp.float32, math.log(0.5), math.log(2.0))), 0.5, 2.0)
    block_list = draw_block_list(jax.random.fold_in(key_list[9], 71), part)
    block_count = draw_block_count(jax.random.fold_in(key_list[9], 71), part)
    taper_class = set_ends(jax.random.randint(key_list[7], (NTILES, KMAX), 0, NCLASS), jax.random.fold_in(key_list[7], 1), 0, NCLASS - 1).astype(jnp.int32)
    taper_table = jnp.clip(jax.random.uniform(key_list[8], (NCLASS,), jnp.float32, 0.1, 1.0), 0.1, 1.0)
    return dict(ensemble=ensemble, predicted=predicted, perturb=perturb, observed=observed, noise_scale=noise_scale, block_list=block_list, block_count=block_count, taper_class=taper_class, taper_table=taper_table)


inflation = 4.0

def solve_tile(routed, tile_x, ids, count, classes, observed, noise_scale, taper_table):
    members = routed.shape[1]
    slots = routed.shape[2]
    width = routed.shape[3]
    table = taper_table.astype(jnp.float32)
    picks = (classes[:, None] == jnp.arange(table.shape[0], dtype=jnp.int32)[None, :]).astype(jnp.float32)
    rho = lax.optimization_barrier(jnp.sum(picks * table[None, :], axis=1))
    used = (jnp.arange(slots, dtype=jnp.int32) < count).astype(jnp.float32)
    weight = jnp.sqrt(rho) * used
    obs_loc = observed.reshape(-1, width)[ids]
    sig_loc = noise_scale.reshape(-1, width)[ids]
    pred = routed[0].astype(jnp.float32)
    pert = routed[1].astype(jnp.float32)
    mean_d = lax.optimization_barrier(jnp.mean(pred, axis=0, keepdims=True))
    zfac = weight[:, None] / (jnp.sqrt((members - 1) * inflation) * sig_loc)
    zmat = ((pred - mean_d) * zfac[None]).astype(jnp.bfloat16).reshape(members, slots * width)
    emat = ((obs_loc[None] - pred) / (jnp.sqrt(inflation) * sig_loc[None]) + pert) * weight[None, :, None]
    emat = emat.astype(jnp.bfloat16).reshape(members, slots * width)
    dims = (((1,), (1,)), ((), ()))
    gram = lax.dot_general(zmat.astype(jnp.float32), zmat.astype(jnp.float32), dims, preferred_element_type=jnp.float32)
    cross = lax.dot_general(zmat.astype(jnp.float32), emat.astype(jnp.float32), dims, preferred_element_type=jnp.float32)
    system = gram + jnp.eye(members, dtype=jnp.float32)
    factor = jnp.linalg.cholesky(system)
    half = lax.linalg.triangular_solve(factor, cross, left_side=True, lower=True)
    solved = lax.linalg.triangular_solve(factor, half, left_side=True, lower=True, transpose_a=True)
    wmat = solved.astype(jnp.bfloat16)
    xf = tile_x.astype(jnp.float32)
    anomaly = ((xf - lax.optimization_barrier(jnp.mean(xf, axis=0, keepdims=True))) / jnp.sqrt(members - 1.0)).astype(jnp.bfloat16)
    delta = lax.dot_general(wmat.astype(jnp.float32), anomaly.astype(jnp.float32), (((0,), (0,)), ((), ())), preferred_element_type=jnp.float32)
    return (xf + delta).astype(jnp.bfloat16)

def reference(ensemble, predicted, perturb, observed, noise_scale, block_list, block_count, taper_class, taper_table):
    members = ensemble.shape[0]
    stacked = jnp.stack([predicted, perturb]).reshape(2, members, NBLK, CB)

    def one_tile(tile):
        ids = block_list[tile]
        routed = jnp.take(stacked, ids, axis=2)
        tile_x = lax.dynamic_slice_in_dim(ensemble, (tile * CT).astype(jnp.int32), CT, 1)
        return solve_tile(routed, tile_x, ids, block_count[tile], taper_class[tile], observed, noise_scale, taper_table)
    tiles = lax.map(one_tile, jnp.arange(NTILES, dtype=jnp.int32))
    return jnp.transpose(tiles, (1, 0, 2)).reshape(members, NTILES * CT)
```

```python
import functools
import jax
import jax.numpy as jnp
from jax import lax
from jax.experimental import pallas as pl
from jax.experimental.pallas import tpu as pltpu
from jax.sharding import PartitionSpec as P

CB = 128
REACH = 2
NBD = 2
BLK = 128
PIV = 4

inflation = 4.0
HIGHEST = lax.Precision.HIGHEST
MESH = pl.DeviceIdType.MESH
REACHED = 2 * REACH + 1
WIDE = 512
CHUNKS = 4
EARLY = 1
VMEM_MIB = 54


def greet(n, me):
    barrier = pltpu.get_barrier_semaphore()

    @pl.loop(1, n)
    def _(i):
        pl.semaphore_signal(
            barrier, inc=1, device_id={"tile": lax.rem(me + i, n)}, device_id_type=MESH
        )

    pl.semaphore_wait(barrier, n - 1)


def blocks_kernel(n, pred_ref, pert_ref, out_ref, own_sem, send_sem, recv_sem, side_send, side_recv):
    me = lax.axis_index("tile")
    width = out_ref.shape[4]
    sources = (pred_ref, pert_ref)
    mine = out_ref.at[REACH]
    greet(n, me)

    def cut(ref, d):
        return ref.at[:, pl.ds(pl.multiple_of(d * width, CB), width)]

    @pl.loop(0, n - 1)
    def _(i):
        d = lax.rem(me + n // 2 + i, n)
        d = jnp.where(d == me, lax.rem(me + n // 2 + n - 1, n), d)
        for kind, ref in enumerate(sources):
            pltpu.make_async_remote_copy(
                src_ref=cut(ref, d),
                dst_ref=mine.at[kind, me],
                send_sem=send_sem.at[kind, d],
                recv_sem=recv_sem.at[kind, me],
                device_id={"tile": d},
                device_id_type=MESH,
            ).start()

    own = [
        pltpu.make_async_copy(cut(ref, me), mine.at[kind, me], own_sem.at[kind])
        for kind, ref in enumerate(sources)
    ]
    for copy in own:
        copy.start()

    @pl.loop(1, n)
    def _(i):
        s = lax.rem(me + i, n)
        for kind, ref in enumerate(sources):
            pltpu.make_async_remote_copy(
                src_ref=cut(ref, s),
                dst_ref=mine.at[kind, s],
                send_sem=send_sem.at[kind, s],
                recv_sem=recv_sem.at[kind, s],
                device_id={"tile": s},
                device_id_type=MESH,
            ).wait()

    for copy in own:
        copy.wait()

    def beside(offset, slot):
        return pltpu.make_async_remote_copy(
            src_ref=mine,
            dst_ref=out_ref.at[slot],
            send_sem=side_send.at[offset + REACH],
            recv_sem=side_recv.at[slot],
            device_id={"tile": me + offset},
            device_id_type=MESH,
        )

    offsets = [o for r in range(REACH, 0, -1) for o in (r, -r)]
    for offset in offsets:

        @pl.when((me + offset >= 0) & (me + offset < n))
        def _(offset=offset):
            beside(offset, REACH - offset).start()

    for offset in offsets:

        @pl.when((me + offset >= 0) & (me + offset < n))
        def _(offset=offset):
            beside(offset, REACH + offset).wait()


def route_blocks(predicted, perturb, n):
    rows, data = predicted.shape
    hbm = pl.BlockSpec(memory_space=pl.ANY)
    sems = pltpu.SemaphoreType.DMA
    out = pl.pallas_call(
        functools.partial(blocks_kernel, n),
        out_shape=jax.ShapeDtypeStruct((REACHED, 2, n, rows, data // n), predicted.dtype),
        in_specs=[hbm, hbm],
        out_specs=hbm,
        scratch_shapes=[sems((2,)), sems((2, n)), sems((2, n)), sems((REACHED,)), sems((REACHED,))],
        compiler_params=pltpu.CompilerParams(collective_id=0, has_side_effects=True),
        cost_estimate=pl.CostEstimate(
            flops=20_000_000_000, bytes_accessed=8_000_000, transcendentals=0
        ),
    )(predicted, perturb)
    return out.reshape(REACHED, 2, n * rows, data // n)


def invert_block(a_ref):
    n = a_ref.shape[0]
    lane = lax.broadcasted_iota(jnp.int32, (1, n), 1)

    def step(q, carry):
        k0 = q * PIV
        a = a_ref[...]
        cols = [
            jnp.take_along_axis(
                a, jnp.full((n, n), k0 + p, jnp.int32), axis=1, mode="promise_in_bounds"
            )
            for p in range(PIV)
        ]
        rows = [a_ref[pl.ds(k0 + p, 1), :] for p in range(PIV)]
        m = [
            [
                jnp.take_along_axis(
                    jnp.broadcast_to(rows[i], (8, n)),
                    jnp.full((8, n), k0 + j, jnp.int32),
                    axis=1,
                    mode="promise_in_bounds",
                )[0:1]
                for j in range(PIV)
            ]
            for i in range(PIV)
        ]
        for p in range(PIV):
            d = 1.0 / m[p][p]
            new = [[None] * PIV for _ in range(PIV)]
            for j in range(PIV):
                new[p][j] = d if j == p else m[p][j] * d
            for i in range(PIV):
                if i == p:
                    continue
                for j in range(PIV):
                    new[i][j] = -m[i][p] * d if j == p else m[i][j] - m[i][p] * new[p][j]
            m = new
        inside = (lane >= k0) & (lane < k0 + PIV)
        rows = [
            jnp.where(inside, jnp.where(lane == k0 + p, 1.0, 0.0), rows[p]) for p in range(PIV)
        ]
        t = []
        for i in range(PIV):
            acc = m[i][0] * rows[0]
            for j in range(1, PIV):
                acc = acc + m[i][j] * rows[j]
            t.append(acc)
        a = jnp.where(inside, 0.0, a)
        for p in range(PIV):
            a = a - cols[p] * t[p]
        a_ref[...] = a
        for p in range(PIV):
            a_ref[pl.ds(k0 + p, 1), :] = t[p]
        return carry

    lax.fori_loop(0, n // PIV, step, 0)


def form_weights(
    list_ref, count_ref, class_ref, table_ref, obs_ref, noise_ref, wt_ref, d_ref, e_in_ref, z_ref, e_ref, s_ref, a_ref
):
    members = wt_ref.shape[0]
    me = lax.axis_index("tile")
    for k in range(list_ref.shape[0]):
        block = jnp.clip(list_ref[k, me], 0, noise_ref.shape[0] - 1)
        slot = jnp.clip(block - (me - REACH) * NBD, 0, REACHED * NBD - 1)
        level = jnp.clip(class_ref[k, me], 0, table_ref.shape[0] - 1)
        rho = jnp.full((1, CB), table_ref[level], jnp.float32)
        used = jnp.full((1, CB), k, jnp.int32) < jnp.full((1, CB), count_ref[me], jnp.int32)
        weight = jnp.where(used, jnp.sqrt(rho), 0.0)
        noise = noise_ref[pl.ds(block, 1), :]
        zfac = weight / (float((members - 1) * inflation) ** 0.5 * noise)
        cols = pl.ds(k * CB, CB)
        pred = d_ref[slot].astype(jnp.float32)
        pert = e_in_ref[slot].astype(jnp.float32)
        mean = jnp.sum(pred, axis=0, keepdims=True) * (1.0 / members)
        z_ref[:, cols] = ((pred - mean) * zfac).astype(jnp.bfloat16)
        e_ref[:, cols] = (
            ((obs_ref[pl.ds(block, 1), :] - pred) / (float(inflation) ** 0.5 * noise) + pert)
            * weight
        ).astype(jnp.bfloat16)
    dims = (((1,), (1,)), ((), ()))
    eye = (
        lax.broadcasted_iota(jnp.int32, (members, members), 0)
        == lax.broadcasted_iota(jnp.int32, (members, members), 1)
    ).astype(jnp.float32)
    s_ref[:, 0:members] = (
        lax.dot_general(z_ref[...], z_ref[...], dims, preferred_element_type=jnp.float32) + eye
    )
    s_ref[:, members:] = lax.dot_general(
        z_ref[...], e_ref[...], dims, preferred_element_type=jnp.float32
    )
    blocks = members // BLK

    def mm(x, y):
        return jnp.dot(x, y, precision=HIGHEST, preferred_element_type=jnp.float32)

    for k in range(blocks):
        lo, hi = k * BLK, (k + 1) * BLK
        a_ref[...] = s_ref[lo:hi, lo:hi]
        invert_block(a_ref)
        upper = mm(a_ref[...], s_ref[lo:hi, hi:])
        s_ref[lo:hi, hi:] = upper
        if k < blocks - 1:
            s_ref[hi:, hi:] -= mm(s_ref[hi:, lo:hi], upper)
    for k in range(blocks - 2, -1, -1):
        lo, hi = k * BLK, (k + 1) * BLK
        s_ref[lo:hi, members:] -= mm(s_ref[lo:hi, hi:members], s_ref[hi:, members:])
    wt_ref[...] = s_ref[:, members:].T.astype(jnp.bfloat16)


def weights_kernel(
    list_ref, count_ref, class_ref, table_ref, obs_ref, noise_ref, beside_ref, wt_ref, *scratch
):
    d_ref, e_in_ref = scratch[:2]
    for i in range(REACHED):
        for b in range(NBD):
            cols = pl.ds(b * CB, CB)
            d_ref[i * NBD + b] = beside_ref[i, 0, :, cols]
            e_in_ref[i * NBD + b] = beside_ref[i, 1, :, cols]
    form_weights(list_ref, count_ref, class_ref, table_ref, obs_ref, noise_ref, wt_ref, *scratch)


def weights_scratch(members, slots):
    return [
        pltpu.VMEM((REACHED * NBD, members, CB), jnp.bfloat16),
        pltpu.VMEM((REACHED * NBD, members, CB), jnp.bfloat16),
        pltpu.VMEM((members, slots * CB), jnp.bfloat16),
        pltpu.VMEM((members, slots * CB), jnp.bfloat16),
        pltpu.VMEM((members, 2 * members), jnp.float32),
        pltpu.VMEM((BLK, BLK), jnp.float32),
    ]


def smoother_kernel(
    n,
    list_hbm,
    count_hbm,
    class_hbm,
    table_hbm,
    obs_hbm,
    noise_hbm,
    pred_ref,
    pert_ref,
    ens_ref,
    out_ref,
    list_ref,
    count_ref,
    class_ref,
    table_ref,
    obs_ref,
    noise_ref,
    beside_ref,
    x_ref,
    stage_ref,
    wt_ref,
    table_sem,
    own_sem,
    block_send,
    block_recv,
    side_send,
    side_recv,
    in_send,
    in_recv,
    out_send,
    out_recv,
    last_sem,
    over_own,
    over_send,
    over_recv,
    *scratch,
):
    me = lax.axis_index("tile")
    members, cells = x_ref.shape
    rows = members // n
    width = beside_ref.shape[4]
    wide = cells // CHUNKS
    scale = 1.0 / float(members - 1) ** 0.5
    sources = (pred_ref, pert_ref)
    mine = beside_ref.at[REACH]

    def cut(ref, d, size):
        return ref.at[:, pl.ds(pl.multiple_of(d * size, CB), size)]

    def held(ref, s):
        return ref.at[pl.ds(pl.multiple_of(s * rows, rows), rows), :]

    def piece(ref, d, c):
        return ref.at[:, pl.ds(pl.multiple_of(d * cells + c * wide, CB), wide)]

    def part(ref, s, c):
        return ref.at[
            pl.ds(pl.multiple_of(s * rows, rows), rows), pl.ds(pl.multiple_of(c * wide, CB), wide)
        ]

    small = (
        (list_hbm, list_ref),
        (count_hbm, count_ref),
        (class_hbm, class_ref),
        (table_hbm, table_ref),
        (obs_hbm, obs_ref),
        (noise_hbm, noise_ref),
    )
    loads = [
        pltpu.make_async_copy(src, dst, table_sem.at[i]) for i, (src, dst) in enumerate(small)
    ]
    own = [
        pltpu.make_async_copy(cut(sources[kind], me, width), mine.at[kind, me], own_sem.at[kind])
        for kind in range(2)
    ]
    own.append(pltpu.make_async_copy(cut(ens_ref, me, cells), held(x_ref, me), own_sem.at[2]))
    for copy in own + loads:
        copy.start()
    greet(n, me)

    def remote(src, dst, send, recv, d):
        return pltpu.make_async_remote_copy(
            src_ref=src,
            dst_ref=dst,
            send_sem=send,
            recv_sem=recv,
            device_id={"tile": d},
            device_id_type=MESH,
        )

    def block(kind, d, s):
        return remote(
            cut(sources[kind], d, width),
            mine.at[kind, s],
            block_send.at[kind, d],
            block_recv.at[kind, s],
            d,
        )

    half = n // 2
    middle = (me >= half - REACH) & (me < half + REACH)
    lacks = jnp.where(me < half, me + REACH, me - REACH)
    place = jnp.where(me < half, 2 * REACH, 0)

    def over(kind, j):
        d = half - REACH + j
        b = d + REACH if j < REACH else d - REACH
        return remote(
            cut(sources[kind], b, width),
            beside_ref.at[2 * REACH if j < REACH else 0, kind, me],
            over_send.at[kind, j],
            over_recv.at[kind, me],
            d,
        )

    def lacking(kind, s):
        return remote(
            cut(sources[kind], lacks, width),
            beside_ref.at[place, kind, s],
            over_send.at[kind, 0],
            over_recv.at[kind, s],
            s,
        )

    def kept(kind):
        return pltpu.make_async_copy(
            cut(sources[kind], lacks, width), beside_ref.at[place, kind, me], over_own.at[kind]
        )

    def arriving(c, d, s):
        return remote(
            piece(ens_ref, d, c), part(x_ref, s, c), in_send.at[c, d], in_recv.at[c, s], d
        )

    def leaving(c, d, s):
        return remote(
            part(stage_ref, d, c), piece(out_ref, s, c), out_send.at[c, d], out_recv.at[c, s], d
        )

    def staying(c):
        return pltpu.make_async_copy(part(stage_ref, me, c), piece(out_ref, me, c), last_sem.at[c])

    def send(first, last):
        @pl.loop(first, last)
        def _(c):
            @pl.loop(1, n)
            def _(i):
                arriving(c, lax.rem(me + i, n), me).start()

    @pl.loop(1, n)
    def _(i):
        for kind in range(2):
            block(kind, lax.rem(me + i, n), me).start()

    for j in range(2 * REACH):

        @pl.when(me != half - REACH + j)
        def _(j=j):
            for kind in range(2):
                over(kind, j).start()

    @pl.when(middle)
    def _():
        for kind in range(2):
            kept(kind).start()

    send(0, EARLY)

    @pl.loop(1, n)
    def _(i):
        s = lax.rem(me + i, n)
        for kind in range(2):
            block(kind, s, s).wait()

    for copy in own[:2]:
        copy.wait()

    odd = lax.rem(me, 2)
    sibling = me + 1 - 2 * odd
    left = (me >= REACH) & ((me < half) | (me >= half + REACH))
    right = (me < n - REACH) & ((me < half - REACH) | (me >= half))

    def side(src, slot, which, d):
        return remote(beside_ref.at[src], beside_ref.at[slot], side_send.at[which], side_recv.at[slot], d)

    pl.when(right)(lambda: side(REACH, 0, 0, me + 2).start())
    pl.when(left)(lambda: side(REACH, 4, 1, me - 2).start())
    side(REACH, 1 + 2 * odd, 2, sibling).start()
    send(EARLY, CHUNKS)

    pl.when(right)(lambda: side(REACH, 4, 0, me + 2).wait())
    pl.when(left)(lambda: side(REACH, 0, 1, me - 2).wait())

    for j in range(2 * REACH):

        @pl.when(me != half - REACH + j)
        def _(j=j):
            for kind in range(2):
                over(kind, j).wait_send()

    @pl.when(middle)
    def _():
        for kind in range(2):
            kept(kind).wait()

        @pl.loop(1, n)
        def _(i):
            for kind in range(2):
                lacking(kind, lax.rem(me + i, n)).wait_recv()

    hands = jnp.where(odd == 1, me, n - 1 - me) >= 2
    gets = jnp.where(odd == 1, n - 1 - me, me) >= 2
    hand = side(4 - 4 * odd, 3 - 2 * odd, 3, sibling)
    got = side(4 - 4 * odd, 1 + 2 * odd, 3, sibling)
    pl.when(hands)(lambda: hand.start())

    side(REACH, 3 - 2 * odd, 2, sibling).wait()
    pl.when(hands)(lambda: hand.wait_send())
    pl.when(gets)(lambda: got.wait_recv())

    d_ref, e_in_ref = scratch[:2]
    for i in range(REACHED):
        for b in range(NBD):
            cols = pl.ds(b * CB, CB)
            d_ref[i * NBD + b] = beside_ref[i, 0, :, :, cols].reshape(members, CB)
            e_in_ref[i * NBD + b] = beside_ref[i, 1, :, :, cols].reshape(members, CB)
    for copy in loads:
        copy.wait()
    form_weights(list_ref, count_ref, class_ref, table_ref, obs_ref, noise_ref, wt_ref, *scratch)
    own[2].wait()

    @pl.loop(0, CHUNKS)
    def _(c):
        @pl.loop(1, n)
        def _(i):
            s = lax.rem(me + i, n)
            arriving(c, s, s).wait()

        @pl.loop(0, wide // WIDE)
        def _(j):
            cols = pl.ds(pl.multiple_of(c * wide + j * WIDE, WIDE), WIDE)
            xf = x_ref[:, cols].astype(jnp.float32)
            mean = jnp.sum(xf, axis=0, keepdims=True) * (1.0 / members)
            anomaly = ((xf - mean) * scale).astype(jnp.bfloat16)
            delta = jnp.dot(wt_ref[...], anomaly, preferred_element_type=jnp.float32)
            stage_ref[:, cols] = (xf + delta).astype(jnp.bfloat16)

        @pl.loop(1, n)
        def _(i):
            leaving(c, lax.rem(me + i, n), me).start()

        staying(c).start()

    @pl.loop(0, CHUNKS)
    def _(c):
        @pl.loop(1, n)
        def _(i):
            s = lax.rem(me + i, n)
            leaving(c, s, s).wait()

        staying(c).wait()


def smooth(tables, predicted, perturb, ensemble, n):
    rows, total = ensemble.shape
    members, cells = rows * n, total // n
    hbm = pl.BlockSpec(memory_space=pl.ANY)
    sems = pltpu.SemaphoreType.DMA
    return pl.pallas_call(
        functools.partial(smoother_kernel, n),
        out_shape=pltpu.VMEM((rows, total), ensemble.dtype),
        in_specs=[hbm] * 9,
        out_specs=hbm,
        scratch_shapes=[
            *[pltpu.SMEM(t.shape, t.dtype) for t in tables[:4]],
            *[pltpu.VMEM(t.shape, t.dtype) for t in tables[4:]],
            pltpu.VMEM((REACHED, 2, n, rows, predicted.shape[1] // n), jnp.bfloat16),
            pltpu.VMEM((members, cells), jnp.bfloat16),
            pltpu.VMEM((members, cells), jnp.bfloat16),
            pltpu.VMEM((members, members), jnp.bfloat16),
            sems((len(tables),)),
            sems((3,)),
            sems((2, n)),
            sems((2, n)),
            sems((4,)),
            sems((REACHED,)),
            sems((CHUNKS, n)),
            sems((CHUNKS, n)),
            sems((CHUNKS, n)),
            sems((CHUNKS, n)),
            sems((CHUNKS,)),
            sems((2,)),
            sems((2, 2 * REACH)),
            sems((2, n)),
            *weights_scratch(members, tables[0].shape[0]),
        ],
        compiler_params=pltpu.CompilerParams(
            collective_id=1, has_side_effects=True, vmem_limit_bytes=VMEM_MIB * 1024 * 1024
        ),
    )(*tables, predicted, perturb, ensemble)


def solve_weights(tables, beside):
    members = beside.shape[2]
    slots = tables[0].shape[0]
    vmem = pl.BlockSpec(memory_space=pltpu.VMEM)
    smem = pl.BlockSpec(memory_space=pltpu.SMEM)
    return pl.pallas_call(
        weights_kernel,
        out_shape=jax.ShapeDtypeStruct((members, members), jnp.bfloat16),
        in_specs=[smem] * 4 + [vmem] * 3,
        out_specs=vmem,
        scratch_shapes=weights_scratch(members, slots),
        compiler_params=pltpu.CompilerParams(vmem_limit_bytes=32 * 1024 * 1024),
        cost_estimate=pl.CostEstimate(
            flops=60_000_000_000, bytes_accessed=8_000_000, transcendentals=0
        ),
    )(*tables, beside)


def per_device(
    ensemble,
    predicted,
    perturb,
    observed,
    noise_scale,
    block_list,
    block_count,
    taper_class,
    taper_table,
):
    n = lax.axis_size("tile")
    members = ensemble.shape[0] * n
    tables = (
        block_list.T,
        block_count,
        taper_class.T,
        taper_table,
        observed.reshape(-1, CB),
        noise_scale.reshape(-1, CB),
    )
    if ensemble.shape[0] % 16 == 0 and n % 8 == 0:
        return smooth(tables, predicted, perturb, ensemble, n)
    beside = route_blocks(predicted, perturb, n)
    beside, ensemble = lax.optimization_barrier((beside, ensemble))
    tile_x = lax.all_to_all(ensemble, "tile", split_axis=1, concat_axis=0, tiled=True)
    wt = solve_weights(tables, beside)
    xf = tile_x.astype(jnp.float32)
    anomaly = ((xf - jnp.mean(xf, axis=0, keepdims=True)) / jnp.sqrt(members - 1.0)).astype(
        jnp.bfloat16
    )
    delta = lax.dot_general(
        wt, anomaly, (((1,), (0,)), ((), ())), preferred_element_type=jnp.float32
    )
    result = (xf + delta).astype(jnp.bfloat16)
    return lax.all_to_all(result, "tile", split_axis=0, concat_axis=1, tiled=True)


def solution(mesh):
    in_specs = (
        P("tile", "slab"),
        P("tile", "slab"),
        P("tile", "slab"),
        P("slab"),
        P("slab"),
        P(),
        P(),
        P(),
        P(),
    )
    out_specs = P("tile", "slab")
    return jax.shard_map(
        per_device, mesh=mesh, in_specs=in_specs, out_specs=out_specs, check_vma=False
    )
```

```python
import functools
import jax
import jax.numpy as jnp
from jax import lax
from jax.experimental import pallas as pl
from jax.experimental.pallas import tpu as pltpu
from jax.sharding import PartitionSpec as P

CB = 128
REACH = 2
NBD = 2
BLK = 128
PIV = 4

inflation = 4.0
HIGHEST = lax.Precision.HIGHEST
MESH = pl.DeviceIdType.MESH
REACHED = 2 * REACH + 1
WIDE = 512
CHUNKS = 4
EARLY = 2
STRIDE = 3
VMEM_MIB = 54


def greet(n, me):
    barrier = pltpu.get_barrier_semaphore()

    @pl.loop(1, n)
    def _(i):
        pl.semaphore_signal(
            barrier, inc=1, device_id={"tile": lax.rem(me + i, n)}, device_id_type=MESH
        )

    pl.semaphore_wait(barrier, n - 1)


def blocks_kernel(n, pred_ref, pert_ref, out_ref, own_sem, send_sem, recv_sem, side_send, side_recv):
    me = lax.axis_index("tile")
    width = out_ref.shape[4]
    sources = (pred_ref, pert_ref)
    mine = out_ref.at[REACH]
    greet(n, me)

    def cut(ref, d):
        return ref.at[:, pl.ds(pl.multiple_of(d * width, CB), width)]

    @pl.loop(0, n - 1)
    def _(i):
        d = lax.rem(me + n // 2 + i, n)
        d = jnp.where(d == me, lax.rem(me + n // 2 + n - 1, n), d)
        for kind, ref in enumerate(sources):
            pltpu.make_async_remote_copy(
                src_ref=cut(ref, d),
                dst_ref=mine.at[kind, me],
                send_sem=send_sem.at[kind, d],
                recv_sem=recv_sem.at[kind, me],
                device_id={"tile": d},
                device_id_type=MESH,
            ).start()

    own = [
        pltpu.make_async_copy(cut(ref, me), mine.at[kind, me], own_sem.at[kind])
        for kind, ref in enumerate(sources)
    ]
    for copy in own:
        copy.start()

    @pl.loop(1, n)
    def _(i):
        s = lax.rem(me + i, n)
        for kind, ref in enumerate(sources):
            pltpu.make_async_remote_copy(
                src_ref=cut(ref, s),
                dst_ref=mine.at[kind, s],
                send_sem=send_sem.at[kind, s],
                recv_sem=recv_sem.at[kind, s],
                device_id={"tile": s},
                device_id_type=MESH,
            ).wait()

    for copy in own:
        copy.wait()

    def beside(offset, slot):
        return pltpu.make_async_remote_copy(
            src_ref=mine,
            dst_ref=out_ref.at[slot],
            send_sem=side_send.at[offset + REACH],
            recv_sem=side_recv.at[slot],
            device_id={"tile": me + offset},
            device_id_type=MESH,
        )

    offsets = [o for r in range(REACH, 0, -1) for o in (r, -r)]
    for offset in offsets:

        @pl.when((me + offset >= 0) & (me + offset < n))
        def _(offset=offset):
            beside(offset, REACH - offset).start()

    for offset in offsets:

        @pl.when((me + offset >= 0) & (me + offset < n))
        def _(offset=offset):
            beside(offset, REACH + offset).wait()


def route_blocks(predicted, perturb, n):
    rows, data = predicted.shape
    hbm = pl.BlockSpec(memory_space=pl.ANY)
    sems = pltpu.SemaphoreType.DMA
    out = pl.pallas_call(
        functools.partial(blocks_kernel, n),
        out_shape=jax.ShapeDtypeStruct((REACHED, 2, n, rows, data // n), predicted.dtype),
        in_specs=[hbm, hbm],
        out_specs=hbm,
        scratch_shapes=[sems((2,)), sems((2, n)), sems((2, n)), sems((REACHED,)), sems((REACHED,))],
        compiler_params=pltpu.CompilerParams(collective_id=0, has_side_effects=True),
        cost_estimate=pl.CostEstimate(
            flops=20_000_000_000, bytes_accessed=8_000_000, transcendentals=0
        ),
    )(predicted, perturb)
    return out.reshape(REACHED, 2, n * rows, data // n)


def invert_block(a_ref):
    n = a_ref.shape[0]
    lane = lax.broadcasted_iota(jnp.int32, (1, n), 1)

    def step(q, carry):
        k0 = q * PIV
        a = a_ref[...]
        cols = [
            jnp.take_along_axis(
                a, jnp.full((n, n), k0 + p, jnp.int32), axis=1, mode="promise_in_bounds"
            )
            for p in range(PIV)
        ]
        rows = [a_ref[pl.ds(k0 + p, 1), :] for p in range(PIV)]
        m = [
            [
                jnp.take_along_axis(
                    jnp.broadcast_to(rows[i], (8, n)),
                    jnp.full((8, n), k0 + j, jnp.int32),
                    axis=1,
                    mode="promise_in_bounds",
                )[0:1]
                for j in range(PIV)
            ]
            for i in range(PIV)
        ]
        for p in range(PIV):
            d = 1.0 / m[p][p]
            new = [[None] * PIV for _ in range(PIV)]
            for j in range(PIV):
                new[p][j] = d if j == p else m[p][j] * d
            for i in range(PIV):
                if i == p:
                    continue
                for j in range(PIV):
                    new[i][j] = -m[i][p] * d if j == p else m[i][j] - m[i][p] * new[p][j]
            m = new
        inside = (lane >= k0) & (lane < k0 + PIV)
        rows = [
            jnp.where(inside, jnp.where(lane == k0 + p, 1.0, 0.0), rows[p]) for p in range(PIV)
        ]
        t = []
        for i in range(PIV):
            acc = m[i][0] * rows[0]
            for j in range(1, PIV):
                acc = acc + m[i][j] * rows[j]
            t.append(acc)
        a = jnp.where(inside, 0.0, a)
        for p in range(PIV):
            a = a - cols[p] * t[p]
        a_ref[...] = a
        for p in range(PIV):
            a_ref[pl.ds(k0 + p, 1), :] = t[p]
        return carry

    lax.fori_loop(0, n // PIV, step, 0)


def form_weights(
    list_ref, count_ref, class_ref, table_ref, obs_ref, noise_ref, wt_ref, d_ref, e_in_ref, z_ref, e_ref, s_ref, a_ref
):
    members = wt_ref.shape[0]
    me = lax.axis_index("tile")
    for k in range(list_ref.shape[0]):
        block = jnp.clip(list_ref[k, me], 0, noise_ref.shape[0] - 1)
        slot = jnp.clip(block - (me - REACH) * NBD, 0, REACHED * NBD - 1)
        level = jnp.clip(class_ref[k, me], 0, table_ref.shape[0] - 1)
        rho = jnp.full((1, CB), table_ref[level], jnp.float32)
        used = jnp.full((1, CB), k, jnp.int32) < jnp.full((1, CB), count_ref[me], jnp.int32)
        weight = jnp.where(used, jnp.sqrt(rho), 0.0)
        noise = noise_ref[pl.ds(block, 1), :]
        zfac = weight / (float((members - 1) * inflation) ** 0.5 * noise)
        cols = pl.ds(k * CB, CB)
        pred = d_ref[slot].astype(jnp.float32)
        pert = e_in_ref[slot].astype(jnp.float32)
        mean = jnp.sum(pred, axis=0, keepdims=True) * (1.0 / members)
        z_ref[:, cols] = ((pred - mean) * zfac).astype(jnp.bfloat16)
        e_ref[:, cols] = (
            ((obs_ref[pl.ds(block, 1), :] - pred) / (float(inflation) ** 0.5 * noise) + pert)
            * weight
        ).astype(jnp.bfloat16)
    dims = (((1,), (1,)), ((), ()))
    eye = (
        lax.broadcasted_iota(jnp.int32, (members, members), 0)
        == lax.broadcasted_iota(jnp.int32, (members, members), 1)
    ).astype(jnp.float32)
    s_ref[:, 0:members] = (
        lax.dot_general(z_ref[...], z_ref[...], dims, preferred_element_type=jnp.float32) + eye
    )
    s_ref[:, members:] = lax.dot_general(
        z_ref[...], e_ref[...], dims, preferred_element_type=jnp.float32
    )
    blocks = members // BLK

    def mm(x, y):
        return jnp.dot(x, y, precision=HIGHEST, preferred_element_type=jnp.float32)

    for k in range(blocks):
        lo, hi = k * BLK, (k + 1) * BLK
        a_ref[...] = s_ref[lo:hi, lo:hi]
        invert_block(a_ref)
        upper = mm(a_ref[...], s_ref[lo:hi, hi:])
        s_ref[lo:hi, hi:] = upper
        if k < blocks - 1:
            s_ref[hi:, hi:] -= mm(s_ref[hi:, lo:hi], upper)
    for k in range(blocks - 2, -1, -1):
        lo, hi = k * BLK, (k + 1) * BLK
        s_ref[lo:hi, members:] -= mm(s_ref[lo:hi, hi:members], s_ref[hi:, members:])
    wt_ref[...] = s_ref[:, members:].T.astype(jnp.bfloat16)


def weights_kernel(
    list_ref, count_ref, class_ref, table_ref, obs_ref, noise_ref, beside_ref, wt_ref, *scratch
):
    d_ref, e_in_ref = scratch[:2]
    for i in range(REACHED):
        for b in range(NBD):
            cols = pl.ds(b * CB, CB)
            d_ref[i * NBD + b] = beside_ref[i, 0, :, cols]
            e_in_ref[i * NBD + b] = beside_ref[i, 1, :, cols]
    form_weights(list_ref, count_ref, class_ref, table_ref, obs_ref, noise_ref, wt_ref, *scratch)


def weights_scratch(members, slots):
    return [
        pltpu.VMEM((REACHED * NBD, members, CB), jnp.bfloat16),
        pltpu.VMEM((REACHED * NBD, members, CB), jnp.bfloat16),
        pltpu.VMEM((members, slots * CB), jnp.bfloat16),
        pltpu.VMEM((members, slots * CB), jnp.bfloat16),
        pltpu.VMEM((members, 2 * members), jnp.float32),
        pltpu.VMEM((BLK, BLK), jnp.float32),
    ]


def smoother_kernel(
    n,
    list_hbm,
    count_hbm,
    class_hbm,
    table_hbm,
    obs_hbm,
    noise_hbm,
    pred_ref,
    pert_ref,
    ens_ref,
    out_ref,
    list_ref,
    count_ref,
    class_ref,
    table_ref,
    obs_ref,
    noise_ref,
    beside_ref,
    x_ref,
    stage_ref,
    wt_ref,
    table_sem,
    own_sem,
    block_send,
    block_recv,
    side_send,
    side_recv,
    in_send,
    in_recv,
    out_send,
    out_recv,
    last_sem,
    over_own,
    over_send,
    over_recv,
    *scratch,
):
    me = lax.axis_index("tile")
    members, cells = x_ref.shape
    rows = members // n
    width = beside_ref.shape[4]
    wide = cells // CHUNKS
    scale = 1.0 / float(members - 1) ** 0.5
    sources = (pred_ref, pert_ref)
    mine = beside_ref.at[REACH]

    def cut(ref, d, size):
        return ref.at[:, pl.ds(pl.multiple_of(d * size, CB), size)]

    def held(ref, s):
        return ref.at[pl.ds(pl.multiple_of(s * rows, rows), rows), :]

    def piece(ref, d, c):
        return ref.at[:, pl.ds(pl.multiple_of(d * cells + c * wide, CB), wide)]

    def part(ref, s, c):
        return ref.at[
            pl.ds(pl.multiple_of(s * rows, rows), rows), pl.ds(pl.multiple_of(c * wide, CB), wide)
        ]

    small = (
        (list_hbm, list_ref),
        (count_hbm, count_ref),
        (class_hbm, class_ref),
        (table_hbm, table_ref),
        (obs_hbm, obs_ref),
        (noise_hbm, noise_ref),
    )
    loads = [
        pltpu.make_async_copy(src, dst, table_sem.at[i]) for i, (src, dst) in enumerate(small)
    ]
    own = [
        pltpu.make_async_copy(cut(sources[kind], me, width), mine.at[kind, me], own_sem.at[kind])
        for kind in range(2)
    ]
    own.append(pltpu.make_async_copy(cut(ens_ref, me, cells), held(x_ref, me), own_sem.at[2]))
    for copy in own + loads:
        copy.start()
    greet(n, me)

    def remote(src, dst, send, recv, d):
        return pltpu.make_async_remote_copy(
            src_ref=src,
            dst_ref=dst,
            send_sem=send,
            recv_sem=recv,
            device_id={"tile": d},
            device_id_type=MESH,
        )

    def block(kind, d, s):
        return remote(
            cut(sources[kind], d, width),
            mine.at[kind, s],
            block_send.at[kind, d],
            block_recv.at[kind, s],
            d,
        )

    half = n // 2
    middle = (me >= half - REACH) & (me < half + REACH)
    lacks = jnp.where(me < half, me + REACH, me - REACH)
    place = jnp.where(me < half, 2 * REACH, 0)

    def over(kind, j):
        d = half - REACH + j
        b = d + REACH if j < REACH else d - REACH
        return remote(
            cut(sources[kind], b, width),
            beside_ref.at[2 * REACH if j < REACH else 0, kind, me],
            over_send.at[kind, j],
            over_recv.at[kind, me],
            d,
        )

    def lacking(kind, s):
        return remote(
            cut(sources[kind], lacks, width),
            beside_ref.at[place, kind, s],
            over_send.at[kind, 0],
            over_recv.at[kind, s],
            s,
        )

    def kept(kind):
        return pltpu.make_async_copy(
            cut(sources[kind], lacks, width), beside_ref.at[place, kind, me], over_own.at[kind]
        )

    def arriving(c, d, s):
        return remote(
            piece(ens_ref, d, c), part(x_ref, s, c), in_send.at[c, d], in_recv.at[c, s], d
        )

    def leaving(c, d, s):
        return remote(
            part(stage_ref, d, c), piece(out_ref, s, c), out_send.at[c, d], out_recv.at[c, s], d
        )

    def staying(c):
        return pltpu.make_async_copy(part(stage_ref, me, c), piece(out_ref, me, c), last_sem.at[c])

    def send(first, last):
        @pl.loop(first, last)
        def _(c):
            @pl.loop(1, n)
            def _(i):
                arriving(c, lax.rem(me + STRIDE * i, n), me).start()

    @pl.loop(1, n)
    def _(i):
        for kind in range(2):
            block(kind, lax.rem(me + STRIDE * i, n), me).start()

    for j in range(2 * REACH):

        @pl.when(me != half - REACH + j)
        def _(j=j):
            for kind in range(2):
                over(kind, j).start()

    @pl.when(middle)
    def _():
        for kind in range(2):
            kept(kind).start()

    send(0, EARLY)

    @pl.loop(1, n)
    def _(i):
        s = lax.rem(me + i, n)
        for kind in range(2):
            block(kind, s, s).wait()

    for copy in own[:2]:
        copy.wait()

    odd = lax.rem(me, 2)
    sibling = me + 1 - 2 * odd
    left = (me >= REACH) & ((me < half) | (me >= half + REACH))
    right = (me < n - REACH) & ((me < half - REACH) | (me >= half))

    def side(src, slot, which, d):
        return remote(beside_ref.at[src], beside_ref.at[slot], side_send.at[which], side_recv.at[slot], d)

    pl.when(right)(lambda: side(REACH, 0, 0, me + 2).start())
    pl.when(left)(lambda: side(REACH, 4, 1, me - 2).start())
    side(REACH, 1 + 2 * odd, 2, sibling).start()
    send(EARLY, CHUNKS)

    pl.when(right)(lambda: side(REACH, 4, 0, me + 2).wait())
    pl.when(left)(lambda: side(REACH, 0, 1, me - 2).wait())

    for j in range(2 * REACH):

        @pl.when(me != half - REACH + j)
        def _(j=j):
            for kind in range(2):
                over(kind, j).wait_send()

    @pl.when(middle)
    def _():
        for kind in range(2):
            kept(kind).wait()

        @pl.loop(1, n)
        def _(i):
            for kind in range(2):
                lacking(kind, lax.rem(me + i, n)).wait_recv()

    hands = jnp.where(odd == 1, me, n - 1 - me) >= 2
    gets = jnp.where(odd == 1, n - 1 - me, me) >= 2
    hand = side(4 - 4 * odd, 3 - 2 * odd, 3, sibling)
    got = side(4 - 4 * odd, 1 + 2 * odd, 3, sibling)
    pl.when(hands)(lambda: hand.start())

    side(REACH, 3 - 2 * odd, 2, sibling).wait()
    pl.when(hands)(lambda: hand.wait_send())
    pl.when(gets)(lambda: got.wait_recv())

    d_ref, e_in_ref = scratch[:2]
    for i in range(REACHED):
        for b in range(NBD):
            cols = pl.ds(b * CB, CB)
            d_ref[i * NBD + b] = beside_ref[i, 0, :, :, cols].reshape(members, CB)
            e_in_ref[i * NBD + b] = beside_ref[i, 1, :, :, cols].reshape(members, CB)
    for copy in loads:
        copy.wait()
    form_weights(list_ref, count_ref, class_ref, table_ref, obs_ref, noise_ref, wt_ref, *scratch)
    own[2].wait()

    @pl.loop(0, CHUNKS)
    def _(c):
        @pl.loop(1, n)
        def _(i):
            s = lax.rem(me + i, n)
            arriving(c, s, s).wait()

        @pl.loop(0, wide // WIDE)
        def _(j):
            cols = pl.ds(pl.multiple_of(c * wide + j * WIDE, WIDE), WIDE)
            xf = x_ref[:, cols].astype(jnp.float32)
            mean = jnp.sum(xf, axis=0, keepdims=True) * (1.0 / members)
            anomaly = ((xf - mean) * scale).astype(jnp.bfloat16)
            delta = jnp.dot(wt_ref[...], anomaly, preferred_element_type=jnp.float32)
            stage_ref[:, cols] = (xf + delta).astype(jnp.bfloat16)

        @pl.loop(1, n)
        def _(i):
            leaving(c, lax.rem(me + STRIDE * i, n), me).start()

        staying(c).start()

    @pl.loop(0, CHUNKS)
    def _(c):
        @pl.loop(1, n)
        def _(i):
            s = lax.rem(me + i, n)
            leaving(c, s, s).wait()

        staying(c).wait()


def smooth(tables, predicted, perturb, ensemble, n):
    rows, total = ensemble.shape
    members, cells = rows * n, total // n
    hbm = pl.BlockSpec(memory_space=pl.ANY)
    sems = pltpu.SemaphoreType.DMA
    return pl.pallas_call(
        functools.partial(smoother_kernel, n),
        out_shape=pltpu.VMEM((rows, total), ensemble.dtype),
        in_specs=[hbm] * 9,
        out_specs=hbm,
        scratch_shapes=[
            *[pltpu.SMEM(t.shape, t.dtype) for t in tables[:4]],
            *[pltpu.VMEM(t.shape, t.dtype) for t in tables[4:]],
            pltpu.VMEM((REACHED, 2, n, rows, predicted.shape[1] // n), jnp.bfloat16),
            pltpu.VMEM((members, cells), jnp.bfloat16),
            pltpu.VMEM((members, cells), jnp.bfloat16),
            pltpu.VMEM((members, members), jnp.bfloat16),
            sems((len(tables),)),
            sems((3,)),
            sems((2, n)),
            sems((2, n)),
            sems((4,)),
            sems((REACHED,)),
            sems((CHUNKS, n)),
            sems((CHUNKS, n)),
            sems((CHUNKS, n)),
            sems((CHUNKS, n)),
            sems((CHUNKS,)),
            sems((2,)),
            sems((2, 2 * REACH)),
            sems((2, n)),
            *weights_scratch(members, tables[0].shape[0]),
        ],
        compiler_params=pltpu.CompilerParams(
            collective_id=1, has_side_effects=True, vmem_limit_bytes=VMEM_MIB * 1024 * 1024
        ),
    )(*tables, predicted, perturb, ensemble)


def solve_weights(tables, beside):
    members = beside.shape[2]
    slots = tables[0].shape[0]
    vmem = pl.BlockSpec(memory_space=pltpu.VMEM)
    smem = pl.BlockSpec(memory_space=pltpu.SMEM)
    return pl.pallas_call(
        weights_kernel,
        out_shape=jax.ShapeDtypeStruct((members, members), jnp.bfloat16),
        in_specs=[smem] * 4 + [vmem] * 3,
        out_specs=vmem,
        scratch_shapes=weights_scratch(members, slots),
        compiler_params=pltpu.CompilerParams(vmem_limit_bytes=32 * 1024 * 1024),
        cost_estimate=pl.CostEstimate(
            flops=60_000_000_000, bytes_accessed=8_000_000, transcendentals=0
        ),
    )(*tables, beside)


def per_device(
    ensemble,
    predicted,
    perturb,
    observed,
    noise_scale,
    block_list,
    block_count,
    taper_class,
    taper_table,
):
    n = lax.axis_size("tile")
    members = ensemble.shape[0] * n
    tables = (
        block_list.T,
        block_count,
        taper_class.T,
        taper_table,
        observed.reshape(-1, CB),
        noise_scale.reshape(-1, CB),
    )
    if ensemble.shape[0] % 16 == 0 and n % 8 == 0:
        return smooth(tables, predicted, perturb, ensemble, n)
    beside = route_blocks(predicted, perturb, n)
    beside, ensemble = lax.optimization_barrier((beside, ensemble))
    tile_x = lax.all_to_all(ensemble, "tile", split_axis=1, concat_axis=0, tiled=True)
    wt = solve_weights(tables, beside)
    xf = tile_x.astype(jnp.float32)
    anomaly = ((xf - jnp.mean(xf, axis=0, keepdims=True)) / jnp.sqrt(members - 1.0)).astype(
        jnp.bfloat16
    )
    delta = lax.dot_general(
        wt, anomaly, (((1,), (0,)), ((), ())), preferred_element_type=jnp.float32
    )
    result = (xf + delta).astype(jnp.bfloat16)
    return lax.all_to_all(result, "tile", split_axis=0, concat_axis=1, tiled=True)


def solution(mesh):
    in_specs = (
        P("tile", "slab"),
        P("tile", "slab"),
        P("tile", "slab"),
        P("slab"),
        P("slab"),
        P(),
        P(),
        P(),
        P(),
    )
    out_specs = P("tile", "slab")
    return jax.shard_map(
        per_device, mesh=mesh, in_specs=in_specs, out_specs=out_specs, check_vma=False
    )
```

```python
import functools
import jax
import jax.numpy as jnp
from jax import lax
from jax.experimental import pallas as pl
from jax.experimental.pallas import tpu as pltpu
from jax.sharding import PartitionSpec as P

CB = 128
REACH = 2
NBD = 2
BLK = 128
PIV = 4

inflation = 4.0
HIGHEST = lax.Precision.HIGHEST
MESH = pl.DeviceIdType.MESH
REACHED = 2 * REACH + 1
WIDE = 512
EIGHTHS = ((2,), (4, 2))
EARLY = 1
STRIDE = 3
VMEM_MIB = 54


def greet(n, me):
    barrier = pltpu.get_barrier_semaphore()

    @pl.loop(1, n)
    def _(i):
        pl.semaphore_signal(
            barrier, inc=1, device_id={"tile": lax.rem(me + i, n)}, device_id_type=MESH
        )

    pl.semaphore_wait(barrier, n - 1)


def blocks_kernel(n, pred_ref, pert_ref, out_ref, own_sem, send_sem, recv_sem, side_send, side_recv):
    me = lax.axis_index("tile")
    width = out_ref.shape[4]
    sources = (pred_ref, pert_ref)
    mine = out_ref.at[REACH]
    greet(n, me)

    def cut(ref, d):
        return ref.at[:, pl.ds(pl.multiple_of(d * width, CB), width)]

    @pl.loop(0, n - 1)
    def _(i):
        d = lax.rem(me + n // 2 + i, n)
        d = jnp.where(d == me, lax.rem(me + n // 2 + n - 1, n), d)
        for kind, ref in enumerate(sources):
            pltpu.make_async_remote_copy(
                src_ref=cut(ref, d),
                dst_ref=mine.at[kind, me],
                send_sem=send_sem.at[kind, d],
                recv_sem=recv_sem.at[kind, me],
                device_id={"tile": d},
                device_id_type=MESH,
            ).start()

    own = [
        pltpu.make_async_copy(cut(ref, me), mine.at[kind, me], own_sem.at[kind])
        for kind, ref in enumerate(sources)
    ]
    for copy in own:
        copy.start()

    @pl.loop(1, n)
    def _(i):
        s = lax.rem(me + i, n)
        for kind, ref in enumerate(sources):
            pltpu.make_async_remote_copy(
                src_ref=cut(ref, s),
                dst_ref=mine.at[kind, s],
                send_sem=send_sem.at[kind, s],
                recv_sem=recv_sem.at[kind, s],
                device_id={"tile": s},
                device_id_type=MESH,
            ).wait()

    for copy in own:
        copy.wait()

    def beside(offset, slot):
        return pltpu.make_async_remote_copy(
            src_ref=mine,
            dst_ref=out_ref.at[slot],
            send_sem=side_send.at[offset + REACH],
            recv_sem=side_recv.at[slot],
            device_id={"tile": me + offset},
            device_id_type=MESH,
        )

    offsets = [o for r in range(REACH, 0, -1) for o in (r, -r)]
    for offset in offsets:

        @pl.when((me + offset >= 0) & (me + offset < n))
        def _(offset=offset):
            beside(offset, REACH - offset).start()

    for offset in offsets:

        @pl.when((me + offset >= 0) & (me + offset < n))
        def _(offset=offset):
            beside(offset, REACH + offset).wait()


def route_blocks(predicted, perturb, n):
    rows, data = predicted.shape
    hbm = pl.BlockSpec(memory_space=pl.ANY)
    sems = pltpu.SemaphoreType.DMA
    out = pl.pallas_call(
        functools.partial(blocks_kernel, n),
        out_shape=jax.ShapeDtypeStruct((REACHED, 2, n, rows, data // n), predicted.dtype),
        in_specs=[hbm, hbm],
        out_specs=hbm,
        scratch_shapes=[sems((2,)), sems((2, n)), sems((2, n)), sems((REACHED,)), sems((REACHED,))],
        compiler_params=pltpu.CompilerParams(collective_id=0, has_side_effects=True),
        cost_estimate=pl.CostEstimate(
            flops=20_000_000_000, bytes_accessed=8_000_000, transcendentals=0
        ),
    )(predicted, perturb)
    return out.reshape(REACHED, 2, n * rows, data // n)


def invert_block(a_ref):
    n = a_ref.shape[0]
    lane = lax.broadcasted_iota(jnp.int32, (1, n), 1)

    def step(q, carry):
        k0 = q * PIV
        a = a_ref[...]
        cols = [
            jnp.take_along_axis(
                a, jnp.full((n, n), k0 + p, jnp.int32), axis=1, mode="promise_in_bounds"
            )
            for p in range(PIV)
        ]
        rows = [a_ref[pl.ds(k0 + p, 1), :] for p in range(PIV)]
        m = [
            [
                jnp.take_along_axis(
                    jnp.broadcast_to(rows[i], (8, n)),
                    jnp.full((8, n), k0 + j, jnp.int32),
                    axis=1,
                    mode="promise_in_bounds",
                )[0:1]
                for j in range(PIV)
            ]
            for i in range(PIV)
        ]
        for p in range(PIV):
            d = 1.0 / m[p][p]
            new = [[None] * PIV for _ in range(PIV)]
            for j in range(PIV):
                new[p][j] = d if j == p else m[p][j] * d
            for i in range(PIV):
                if i == p:
                    continue
                for j in range(PIV):
                    new[i][j] = -m[i][p] * d if j == p else m[i][j] - m[i][p] * new[p][j]
            m = new
        inside = (lane >= k0) & (lane < k0 + PIV)
        rows = [
            jnp.where(inside, jnp.where(lane == k0 + p, 1.0, 0.0), rows[p]) for p in range(PIV)
        ]
        t = []
        for i in range(PIV):
            acc = m[i][0] * rows[0]
            for j in range(1, PIV):
                acc = acc + m[i][j] * rows[j]
            t.append(acc)
        a = jnp.where(inside, 0.0, a)
        for p in range(PIV):
            a = a - cols[p] * t[p]
        a_ref[...] = a
        for p in range(PIV):
            a_ref[pl.ds(k0 + p, 1), :] = t[p]
        return carry

    lax.fori_loop(0, n // PIV, step, 0)


def form_weights(
    list_ref, count_ref, class_ref, table_ref, obs_ref, noise_ref, wt_ref, d_ref, e_in_ref, z_ref, e_ref, s_ref, a_ref
):
    members = wt_ref.shape[0]
    me = lax.axis_index("tile")
    for k in range(list_ref.shape[0]):
        block = jnp.clip(list_ref[k, me], 0, noise_ref.shape[0] - 1)
        slot = jnp.clip(block - (me - REACH) * NBD, 0, REACHED * NBD - 1)
        level = jnp.clip(class_ref[k, me], 0, table_ref.shape[0] - 1)
        rho = jnp.full((1, CB), table_ref[level], jnp.float32)
        used = jnp.full((1, CB), k, jnp.int32) < jnp.full((1, CB), count_ref[me], jnp.int32)
        weight = jnp.where(used, jnp.sqrt(rho), 0.0)
        noise = noise_ref[pl.ds(block, 1), :]
        zfac = weight / (float((members - 1) * inflation) ** 0.5 * noise)
        cols = pl.ds(k * CB, CB)
        pred = d_ref[slot].astype(jnp.float32)
        pert = e_in_ref[slot].astype(jnp.float32)
        mean = jnp.sum(pred, axis=0, keepdims=True) * (1.0 / members)
        z_ref[:, cols] = ((pred - mean) * zfac).astype(jnp.bfloat16)
        e_ref[:, cols] = (
            ((obs_ref[pl.ds(block, 1), :] - pred) / (float(inflation) ** 0.5 * noise) + pert)
            * weight
        ).astype(jnp.bfloat16)
    dims = (((1,), (1,)), ((), ()))
    eye = (
        lax.broadcasted_iota(jnp.int32, (members, members), 0)
        == lax.broadcasted_iota(jnp.int32, (members, members), 1)
    ).astype(jnp.float32)
    s_ref[:, 0:members] = (
        lax.dot_general(z_ref[...], z_ref[...], dims, preferred_element_type=jnp.float32) + eye
    )
    s_ref[:, members:] = lax.dot_general(
        z_ref[...], e_ref[...], dims, preferred_element_type=jnp.float32
    )
    blocks = members // BLK

    def mm(x, y):
        return jnp.dot(x, y, precision=HIGHEST, preferred_element_type=jnp.float32)

    for k in range(blocks):
        lo, hi = k * BLK, (k + 1) * BLK
        a_ref[...] = s_ref[lo:hi, lo:hi]
        invert_block(a_ref)
        upper = mm(a_ref[...], s_ref[lo:hi, hi:])
        s_ref[lo:hi, hi:] = upper
        if k < blocks - 1:
            s_ref[hi:, hi:] -= mm(s_ref[hi:, lo:hi], upper)
    for k in range(blocks - 2, -1, -1):
        lo, hi = k * BLK, (k + 1) * BLK
        s_ref[lo:hi, members:] -= mm(s_ref[lo:hi, hi:members], s_ref[hi:, members:])
    wt_ref[...] = s_ref[:, members:].T.astype(jnp.bfloat16)


def weights_kernel(
    list_ref, count_ref, class_ref, table_ref, obs_ref, noise_ref, beside_ref, wt_ref, *scratch
):
    d_ref, e_in_ref = scratch[:2]
    for i in range(REACHED):
        for b in range(NBD):
            cols = pl.ds(b * CB, CB)
            d_ref[i * NBD + b] = beside_ref[i, 0, :, cols]
            e_in_ref[i * NBD + b] = beside_ref[i, 1, :, cols]
    form_weights(list_ref, count_ref, class_ref, table_ref, obs_ref, noise_ref, wt_ref, *scratch)


def weights_scratch(members, slots):
    return [
        pltpu.VMEM((REACHED * NBD, members, CB), jnp.bfloat16),
        pltpu.VMEM((REACHED * NBD, members, CB), jnp.bfloat16),
        pltpu.VMEM((members, slots * CB), jnp.bfloat16),
        pltpu.VMEM((members, slots * CB), jnp.bfloat16),
        pltpu.VMEM((members, 2 * members), jnp.float32),
        pltpu.VMEM((BLK, BLK), jnp.float32),
    ]


def smoother_kernel(
    n,
    list_hbm,
    count_hbm,
    class_hbm,
    table_hbm,
    obs_hbm,
    noise_hbm,
    pred_ref,
    pert_ref,
    ens_ref,
    out_ref,
    list_ref,
    count_ref,
    class_ref,
    table_ref,
    obs_ref,
    noise_ref,
    beside_ref,
    x_ref,
    stage_ref,
    wt_ref,
    table_sem,
    own_sem,
    block_send,
    block_recv,
    side_send,
    side_recv,
    in_send,
    in_recv,
    out_send,
    out_recv,
    last_sem,
    over_own,
    over_send,
    over_recv,
    *scratch,
):
    me = lax.axis_index("tile")
    members, cells = x_ref.shape
    rows = members // n
    width = beside_ref.shape[4]
    unit = cells // 8
    parts, pieces = [], []
    for group in EIGHTHS:
        first = sum(w for _, w in parts)
        parts.append((first, sum(group) * unit))
        for w in group:
            pieces.append((first, w * unit, len(parts) - 1))
            first += w * unit
    scale = 1.0 / float(members - 1) ** 0.5
    sources = (pred_ref, pert_ref)
    mine = beside_ref.at[REACH]

    def cut(ref, d, size):
        return ref.at[:, pl.ds(pl.multiple_of(d * size, CB), size)]

    def held(ref, s):
        return ref.at[pl.ds(pl.multiple_of(s * rows, rows), rows), :]

    def across(ref, d, first, wide):
        return ref.at[:, pl.ds(pl.multiple_of(d * cells + first, CB), wide)]

    def down(ref, s, first, wide):
        return ref.at[pl.ds(pl.multiple_of(s * rows, rows), rows), pl.ds(first, wide)]

    small = (
        (list_hbm, list_ref),
        (count_hbm, count_ref),
        (class_hbm, class_ref),
        (table_hbm, table_ref),
        (obs_hbm, obs_ref),
        (noise_hbm, noise_ref),
    )
    loads = [
        pltpu.make_async_copy(src, dst, table_sem.at[i]) for i, (src, dst) in enumerate(small)
    ]
    own = [
        pltpu.make_async_copy(cut(sources[kind], me, width), mine.at[kind, me], own_sem.at[kind])
        for kind in range(2)
    ]
    own.append(pltpu.make_async_copy(cut(ens_ref, me, cells), held(x_ref, me), own_sem.at[2]))
    for copy in own + loads:
        copy.start()
    greet(n, me)

    def remote(src, dst, send, recv, d):
        return pltpu.make_async_remote_copy(
            src_ref=src,
            dst_ref=dst,
            send_sem=send,
            recv_sem=recv,
            device_id={"tile": d},
            device_id_type=MESH,
        )

    def block(kind, d, s):
        return remote(
            cut(sources[kind], d, width),
            mine.at[kind, s],
            block_send.at[kind, d],
            block_recv.at[kind, s],
            d,
        )

    half = n // 2
    middle = (me >= half - REACH) & (me < half + REACH)
    lacks = jnp.where(me < half, me + REACH, me - REACH)
    place = jnp.where(me < half, 2 * REACH, 0)

    def over(kind, j):
        d = half - REACH + j
        b = d + REACH if j < REACH else d - REACH
        return remote(
            cut(sources[kind], b, width),
            beside_ref.at[2 * REACH if j < REACH else 0, kind, me],
            over_send.at[kind, j],
            over_recv.at[kind, me],
            d,
        )

    def lacking(kind, s):
        return remote(
            cut(sources[kind], lacks, width),
            beside_ref.at[place, kind, s],
            over_send.at[kind, 0],
            over_recv.at[kind, s],
            s,
        )

    def kept(kind):
        return pltpu.make_async_copy(
            cut(sources[kind], lacks, width), beside_ref.at[place, kind, me], over_own.at[kind]
        )

    def arriving(c, d, s):
        return remote(
            across(ens_ref, d, *parts[c]),
            down(x_ref, s, *parts[c]),
            in_send.at[c, d],
            in_recv.at[c, s],
            d,
        )

    def leaving(c, d, s):
        return remote(
            down(stage_ref, d, *pieces[c][:2]),
            across(out_ref, s, *pieces[c][:2]),
            out_send.at[c, d],
            out_recv.at[c, s],
            d,
        )

    def staying(c):
        return pltpu.make_async_copy(
            down(stage_ref, me, *pieces[c][:2]), across(out_ref, me, *pieces[c][:2]), last_sem.at[c]
        )

    def send(first, last):
        for c in range(first, last):

            @pl.loop(1, n)
            def _(i, c=c):
                arriving(c, lax.rem(me + STRIDE * i, n), me).start()

    @pl.loop(1, n)
    def _(i):
        for kind in range(2):
            block(kind, lax.rem(me + STRIDE * i, n), me).start()

    for j in range(2 * REACH):

        @pl.when(me != half - REACH + j)
        def _(j=j):
            for kind in range(2):
                over(kind, j).start()

    @pl.when(middle)
    def _():
        for kind in range(2):
            kept(kind).start()

    send(0, EARLY)

    @pl.loop(1, n)
    def _(i):
        s = lax.rem(me + i, n)
        for kind in range(2):
            block(kind, s, s).wait()

    for copy in own[:2]:
        copy.wait()

    odd = lax.rem(me, 2)
    sibling = me + 1 - 2 * odd
    left = (me >= REACH) & ((me < half) | (me >= half + REACH))
    right = (me < n - REACH) & ((me < half - REACH) | (me >= half))

    def side(src, slot, which, d):
        return remote(beside_ref.at[src], beside_ref.at[slot], side_send.at[which], side_recv.at[slot], d)

    pl.when(right)(lambda: side(REACH, 0, 0, me + 2).start())
    pl.when(left)(lambda: side(REACH, 4, 1, me - 2).start())
    side(REACH, 1 + 2 * odd, 2, sibling).start()
    send(EARLY, len(parts))

    pl.when(right)(lambda: side(REACH, 4, 0, me + 2).wait())
    pl.when(left)(lambda: side(REACH, 0, 1, me - 2).wait())

    for j in range(2 * REACH):

        @pl.when(me != half - REACH + j)
        def _(j=j):
            for kind in range(2):
                over(kind, j).wait_send()

    @pl.when(middle)
    def _():
        for kind in range(2):
            kept(kind).wait()

        @pl.loop(1, n)
        def _(i):
            for kind in range(2):
                lacking(kind, lax.rem(me + i, n)).wait_recv()

    hands = jnp.where(odd == 1, me, n - 1 - me) >= 2
    gets = jnp.where(odd == 1, n - 1 - me, me) >= 2
    hand = side(4 - 4 * odd, 3 - 2 * odd, 3, sibling)
    got = side(4 - 4 * odd, 1 + 2 * odd, 3, sibling)
    pl.when(hands)(lambda: hand.start())

    side(REACH, 3 - 2 * odd, 2, sibling).wait()
    pl.when(hands)(lambda: hand.wait_send())
    pl.when(gets)(lambda: got.wait_recv())

    d_ref, e_in_ref = scratch[:2]
    for i in range(REACHED):
        for b in range(NBD):
            cols = pl.ds(b * CB, CB)
            d_ref[i * NBD + b] = beside_ref[i, 0, :, :, cols].reshape(members, CB)
            e_in_ref[i * NBD + b] = beside_ref[i, 1, :, :, cols].reshape(members, CB)
    for copy in loads:
        copy.wait()
    form_weights(list_ref, count_ref, class_ref, table_ref, obs_ref, noise_ref, wt_ref, *scratch)
    own[2].wait()

    there = -1
    for q, (first, wide, c) in enumerate(pieces):
        if c > there:
            there = c

            @pl.loop(1, n)
            def _(i, c=c):
                s = lax.rem(me + i, n)
                arriving(c, s, s).wait()

        @pl.loop(0, wide // WIDE)
        def _(j, first=first):
            cols = pl.ds(pl.multiple_of(first + j * WIDE, WIDE), WIDE)
            xf = x_ref[:, cols].astype(jnp.float32)
            mean = jnp.sum(xf, axis=0, keepdims=True) * (1.0 / members)
            anomaly = ((xf - mean) * scale).astype(jnp.bfloat16)
            delta = jnp.dot(wt_ref[...], anomaly, preferred_element_type=jnp.float32)
            stage_ref[:, cols] = (xf + delta).astype(jnp.bfloat16)

        @pl.loop(1, n)
        def _(i, q=q):
            leaving(q, lax.rem(me + STRIDE * i, n), me).start()

        staying(q).start()

    for q in range(len(pieces)):

        @pl.loop(1, n)
        def _(i, q=q):
            s = lax.rem(me + i, n)
            leaving(q, s, s).wait()

        staying(q).wait()


def smooth(tables, predicted, perturb, ensemble, n):
    rows, total = ensemble.shape
    members, cells = rows * n, total // n
    outs = sum(len(group) for group in EIGHTHS)
    hbm = pl.BlockSpec(memory_space=pl.ANY)
    sems = pltpu.SemaphoreType.DMA
    return pl.pallas_call(
        functools.partial(smoother_kernel, n),
        out_shape=pltpu.VMEM((rows, total), ensemble.dtype),
        in_specs=[hbm] * 9,
        out_specs=hbm,
        scratch_shapes=[
            *[pltpu.SMEM(t.shape, t.dtype) for t in tables[:4]],
            *[pltpu.VMEM(t.shape, t.dtype) for t in tables[4:]],
            pltpu.VMEM((REACHED, 2, n, rows, predicted.shape[1] // n), jnp.bfloat16),
            pltpu.VMEM((members, cells), jnp.bfloat16),
            pltpu.VMEM((members, cells), jnp.bfloat16),
            pltpu.VMEM((members, members), jnp.bfloat16),
            sems((len(tables),)),
            sems((3,)),
            sems((2, n)),
            sems((2, n)),
            sems((4,)),
            sems((REACHED,)),
            sems((len(EIGHTHS), n)),
            sems((len(EIGHTHS), n)),
            sems((outs, n)),
            sems((outs, n)),
            sems((outs,)),
            sems((2,)),
            sems((2, 2 * REACH)),
            sems((2, n)),
            *weights_scratch(members, tables[0].shape[0]),
        ],
        compiler_params=pltpu.CompilerParams(
            collective_id=1, has_side_effects=True, vmem_limit_bytes=VMEM_MIB * 1024 * 1024
        ),
    )(*tables, predicted, perturb, ensemble)


def solve_weights(tables, beside):
    members = beside.shape[2]
    slots = tables[0].shape[0]
    vmem = pl.BlockSpec(memory_space=pltpu.VMEM)
    smem = pl.BlockSpec(memory_space=pltpu.SMEM)
    return pl.pallas_call(
        weights_kernel,
        out_shape=jax.ShapeDtypeStruct((members, members), jnp.bfloat16),
        in_specs=[smem] * 4 + [vmem] * 3,
        out_specs=vmem,
        scratch_shapes=weights_scratch(members, slots),
        compiler_params=pltpu.CompilerParams(vmem_limit_bytes=32 * 1024 * 1024),
        cost_estimate=pl.CostEstimate(
            flops=60_000_000_000, bytes_accessed=8_000_000, transcendentals=0
        ),
    )(*tables, beside)


def per_device(
    ensemble,
    predicted,
    perturb,
    observed,
    noise_scale,
    block_list,
    block_count,
    taper_class,
    taper_table,
):
    n = lax.axis_size("tile")
    members = ensemble.shape[0] * n
    tables = (
        block_list.T,
        block_count,
        taper_class.T,
        taper_table,
        observed.reshape(-1, CB),
        noise_scale.reshape(-1, CB),
    )
    if ensemble.shape[0] % 16 == 0 and n % 8 == 0:
        return smooth(tables, predicted, perturb, ensemble, n)
    beside = route_blocks(predicted, perturb, n)
    beside, ensemble = lax.optimization_barrier((beside, ensemble))
    tile_x = lax.all_to_all(ensemble, "tile", split_axis=1, concat_axis=0, tiled=True)
    wt = solve_weights(tables, beside)
    xf = tile_x.astype(jnp.float32)
    anomaly = ((xf - jnp.mean(xf, axis=0, keepdims=True)) / jnp.sqrt(members - 1.0)).astype(
        jnp.bfloat16
    )
    delta = lax.dot_general(
        wt, anomaly, (((1,), (0,)), ((), ())), preferred_element_type=jnp.float32
    )
    result = (xf + delta).astype(jnp.bfloat16)
    return lax.all_to_all(result, "tile", split_axis=0, concat_axis=1, tiled=True)


def solution(mesh):
    in_specs = (
        P("tile", "slab"),
        P("tile", "slab"),
        P("tile", "slab"),
        P("slab"),
        P("slab"),
        P(),
        P(),
        P(),
        P(),
    )
    out_specs = P("tile", "slab")
    return jax.shard_map(
        per_device, mesh=mesh, in_specs=in_specs, out_specs=out_specs, check_vma=False
    )
```

```python
import functools
import jax
import jax.numpy as jnp
from jax import lax
from jax.experimental import pallas as pl
from jax.experimental.pallas import tpu as pltpu
from jax.sharding import PartitionSpec as P

CB = 128
REACH = 2
NBD = 2
BLK = 128
PIV = 4

inflation = 4.0
HIGHEST = lax.Precision.HIGHEST
MESH = pl.DeviceIdType.MESH
REACHED = 2 * REACH + 1
WIDE = 512
EIGHTHS = ((2,), (6,))
EARLY = 1
STRIDE = 3
VMEM_MIB = 54


def greet(n, me):
    barrier = pltpu.get_barrier_semaphore()

    @pl.loop(1, n)
    def _(i):
        pl.semaphore_signal(
            barrier, inc=1, device_id={"tile": lax.rem(me + i, n)}, device_id_type=MESH
        )

    pl.semaphore_wait(barrier, n - 1)


def blocks_kernel(n, pred_ref, pert_ref, out_ref, own_sem, send_sem, recv_sem, side_send, side_recv):
    me = lax.axis_index("tile")
    width = out_ref.shape[4]
    sources = (pred_ref, pert_ref)
    mine = out_ref.at[REACH]
    greet(n, me)

    def cut(ref, d):
        return ref.at[:, pl.ds(pl.multiple_of(d * width, CB), width)]

    @pl.loop(0, n - 1)
    def _(i):
        d = lax.rem(me + n // 2 + i, n)
        d = jnp.where(d == me, lax.rem(me + n // 2 + n - 1, n), d)
        for kind, ref in enumerate(sources):
            pltpu.make_async_remote_copy(
                src_ref=cut(ref, d),
                dst_ref=mine.at[kind, me],
                send_sem=send_sem.at[kind, d],
                recv_sem=recv_sem.at[kind, me],
                device_id={"tile": d},
                device_id_type=MESH,
            ).start()

    own = [
        pltpu.make_async_copy(cut(ref, me), mine.at[kind, me], own_sem.at[kind])
        for kind, ref in enumerate(sources)
    ]
    for copy in own:
        copy.start()

    @pl.loop(1, n)
    def _(i):
        s = lax.rem(me + i, n)
        for kind, ref in enumerate(sources):
            pltpu.make_async_remote_copy(
                src_ref=cut(ref, s),
                dst_ref=mine.at[kind, s],
                send_sem=send_sem.at[kind, s],
                recv_sem=recv_sem.at[kind, s],
                device_id={"tile": s},
                device_id_type=MESH,
            ).wait()

    for copy in own:
        copy.wait()

    def beside(offset, slot):
        return pltpu.make_async_remote_copy(
            src_ref=mine,
            dst_ref=out_ref.at[slot],
            send_sem=side_send.at[offset + REACH],
            recv_sem=side_recv.at[slot],
            device_id={"tile": me + offset},
            device_id_type=MESH,
        )

    offsets = [o for r in range(REACH, 0, -1) for o in (r, -r)]
    for offset in offsets:

        @pl.when((me + offset >= 0) & (me + offset < n))
        def _(offset=offset):
            beside(offset, REACH - offset).start()

    for offset in offsets:

        @pl.when((me + offset >= 0) & (me + offset < n))
        def _(offset=offset):
            beside(offset, REACH + offset).wait()


def route_blocks(predicted, perturb, n):
    rows, data = predicted.shape
    hbm = pl.BlockSpec(memory_space=pl.ANY)
    sems = pltpu.SemaphoreType.DMA
    out = pl.pallas_call(
        functools.partial(blocks_kernel, n),
        out_shape=jax.ShapeDtypeStruct((REACHED, 2, n, rows, data // n), predicted.dtype),
        in_specs=[hbm, hbm],
        out_specs=hbm,
        scratch_shapes=[sems((2,)), sems((2, n)), sems((2, n)), sems((REACHED,)), sems((REACHED,))],
        compiler_params=pltpu.CompilerParams(collective_id=0, has_side_effects=True),
        cost_estimate=pl.CostEstimate(
            flops=20_000_000_000, bytes_accessed=8_000_000, transcendentals=0
        ),
    )(predicted, perturb)
    return out.reshape(REACHED, 2, n * rows, data // n)


def invert_block(a_ref):
    n = a_ref.shape[0]
    lane = lax.broadcasted_iota(jnp.int32, (1, n), 1)

    def step(q, carry):
        k0 = q * PIV
        a = a_ref[...]
        cols = [
            jnp.take_along_axis(
                a, jnp.full((n, n), k0 + p, jnp.int32), axis=1, mode="promise_in_bounds"
            )
            for p in range(PIV)
        ]
        rows = [a_ref[pl.ds(k0 + p, 1), :] for p in range(PIV)]
        m = [
            [
                jnp.take_along_axis(
                    jnp.broadcast_to(rows[i], (8, n)),
                    jnp.full((8, n), k0 + j, jnp.int32),
                    axis=1,
                    mode="promise_in_bounds",
                )[0:1]
                for j in range(PIV)
            ]
            for i in range(PIV)
        ]
        for p in range(PIV):
            d = 1.0 / m[p][p]
            new = [[None] * PIV for _ in range(PIV)]
            for j in range(PIV):
                new[p][j] = d if j == p else m[p][j] * d
            for i in range(PIV):
                if i == p:
                    continue
                for j in range(PIV):
                    new[i][j] = -m[i][p] * d if j == p else m[i][j] - m[i][p] * new[p][j]
            m = new
        inside = (lane >= k0) & (lane < k0 + PIV)
        rows = [
            jnp.where(inside, jnp.where(lane == k0 + p, 1.0, 0.0), rows[p]) for p in range(PIV)
        ]
        t = []
        for i in range(PIV):
            acc = m[i][0] * rows[0]
            for j in range(1, PIV):
                acc = acc + m[i][j] * rows[j]
            t.append(acc)
        a = jnp.where(inside, 0.0, a)
        for p in range(PIV):
            a = a - cols[p] * t[p]
        a_ref[...] = a
        for p in range(PIV):
            a_ref[pl.ds(k0 + p, 1), :] = t[p]
        return carry

    lax.fori_loop(0, n // PIV, step, 0)


def form_weights(
    list_ref, count_ref, class_ref, table_ref, obs_ref, noise_ref, wt_ref, d_ref, e_in_ref, z_ref, e_ref, s_ref, a_ref
):
    members = wt_ref.shape[0]
    me = lax.axis_index("tile")
    for k in range(list_ref.shape[0]):
        block = jnp.clip(list_ref[k, me], 0, noise_ref.shape[0] - 1)
        slot = jnp.clip(block - (me - REACH) * NBD, 0, REACHED * NBD - 1)
        level = jnp.clip(class_ref[k, me], 0, table_ref.shape[0] - 1)
        rho = jnp.full((1, CB), table_ref[level], jnp.float32)
        used = jnp.full((1, CB), k, jnp.int32) < jnp.full((1, CB), count_ref[me], jnp.int32)
        weight = jnp.where(used, jnp.sqrt(rho), 0.0)
        noise = noise_ref[pl.ds(block, 1), :]
        zfac = weight / (float((members - 1) * inflation) ** 0.5 * noise)
        cols = pl.ds(k * CB, CB)
        pred = d_ref[slot].astype(jnp.float32)
        pert = e_in_ref[slot].astype(jnp.float32)
        mean = jnp.sum(pred, axis=0, keepdims=True) * (1.0 / members)
        z_ref[:, cols] = ((pred - mean) * zfac).astype(jnp.bfloat16)
        e_ref[:, cols] = (
            ((obs_ref[pl.ds(block, 1), :] - pred) / (float(inflation) ** 0.5 * noise) + pert)
            * weight
        ).astype(jnp.bfloat16)
    dims = (((1,), (1,)), ((), ()))
    eye = (
        lax.broadcasted_iota(jnp.int32, (members, members), 0)
        == lax.broadcasted_iota(jnp.int32, (members, members), 1)
    ).astype(jnp.float32)
    s_ref[:, 0:members] = (
        lax.dot_general(z_ref[...], z_ref[...], dims, preferred_element_type=jnp.float32) + eye
    )
    s_ref[:, members:] = lax.dot_general(
        z_ref[...], e_ref[...], dims, preferred_element_type=jnp.float32
    )
    blocks = members // BLK

    def mm(x, y):
        return jnp.dot(x, y, precision=HIGHEST, preferred_element_type=jnp.float32)

    for k in range(blocks):
        lo, hi = k * BLK, (k + 1) * BLK
        a_ref[...] = s_ref[lo:hi, lo:hi]
        invert_block(a_ref)
        upper = mm(a_ref[...], s_ref[lo:hi, hi:])
        s_ref[lo:hi, hi:] = upper
        if k < blocks - 1:
            s_ref[hi:, hi:] -= mm(s_ref[hi:, lo:hi], upper)
    for k in range(blocks - 2, -1, -1):
        lo, hi = k * BLK, (k + 1) * BLK
        s_ref[lo:hi, members:] -= mm(s_ref[lo:hi, hi:members], s_ref[hi:, members:])
    wt_ref[...] = s_ref[:, members:].T.astype(jnp.bfloat16)


def weights_kernel(
    list_ref, count_ref, class_ref, table_ref, obs_ref, noise_ref, beside_ref, wt_ref, *scratch
):
    d_ref, e_in_ref = scratch[:2]
    for i in range(REACHED):
        for b in range(NBD):
            cols = pl.ds(b * CB, CB)
            d_ref[i * NBD + b] = beside_ref[i, 0, :, cols]
            e_in_ref[i * NBD + b] = beside_ref[i, 1, :, cols]
    form_weights(list_ref, count_ref, class_ref, table_ref, obs_ref, noise_ref, wt_ref, *scratch)


def weights_scratch(members, slots):
    return [
        pltpu.VMEM((REACHED * NBD, members, CB), jnp.bfloat16),
        pltpu.VMEM((REACHED * NBD, members, CB), jnp.bfloat16),
        pltpu.VMEM((members, slots * CB), jnp.bfloat16),
        pltpu.VMEM((members, slots * CB), jnp.bfloat16),
        pltpu.VMEM((members, 2 * members), jnp.float32),
        pltpu.VMEM((BLK, BLK), jnp.float32),
    ]


def smoother_kernel(
    n,
    list_hbm,
    count_hbm,
    class_hbm,
    table_hbm,
    obs_hbm,
    noise_hbm,
    pred_ref,
    pert_ref,
    ens_ref,
    out_ref,
    list_ref,
    count_ref,
    class_ref,
    table_ref,
    obs_ref,
    noise_ref,
    beside_ref,
    x_ref,
    stage_ref,
    wt_ref,
    table_sem,
    own_sem,
    block_send,
    block_recv,
    side_send,
    side_recv,
    in_send,
    in_recv,
    out_send,
    out_recv,
    last_sem,
    over_own,
    over_send,
    over_recv,
    *scratch,
):
    me = lax.axis_index("tile")
    members, cells = x_ref.shape
    rows = members // n
    width = beside_ref.shape[4]
    unit = cells // 8
    parts, pieces = [], []
    for group in EIGHTHS:
        first = sum(w for _, w in parts)
        parts.append((first, sum(group) * unit))
        for w in group:
            pieces.append((first, w * unit, len(parts) - 1))
            first += w * unit
    scale = 1.0 / float(members - 1) ** 0.5
    sources = (pred_ref, pert_ref)
    mine = beside_ref.at[REACH]

    def cut(ref, d, size):
        return ref.at[:, pl.ds(pl.multiple_of(d * size, CB), size)]

    def held(ref, s):
        return ref.at[pl.ds(pl.multiple_of(s * rows, rows), rows), :]

    def across(ref, d, first, wide):
        return ref.at[:, pl.ds(pl.multiple_of(d * cells + first, CB), wide)]

    def down(ref, s, first, wide):
        return ref.at[pl.ds(pl.multiple_of(s * rows, rows), rows), pl.ds(first, wide)]

    small = (
        (list_hbm, list_ref),
        (count_hbm, count_ref),
        (class_hbm, class_ref),
        (table_hbm, table_ref),
        (obs_hbm, obs_ref),
        (noise_hbm, noise_ref),
    )
    loads = [
        pltpu.make_async_copy(src, dst, table_sem.at[i]) for i, (src, dst) in enumerate(small)
    ]
    own = [
        pltpu.make_async_copy(cut(sources[kind], me, width), mine.at[kind, me], own_sem.at[kind])
        for kind in range(2)
    ]
    own.append(pltpu.make_async_copy(cut(ens_ref, me, cells), held(x_ref, me), own_sem.at[2]))
    for copy in own + loads:
        copy.start()
    greet(n, me)

    def remote(src, dst, send, recv, d):
        return pltpu.make_async_remote_copy(
            src_ref=src,
            dst_ref=dst,
            send_sem=send,
            recv_sem=recv,
            device_id={"tile": d},
            device_id_type=MESH,
        )

    def block(kind, d, s):
        return remote(
            cut(sources[kind], d, width),
            mine.at[kind, s],
            block_send.at[kind, d],
            block_recv.at[kind, s],
            d,
        )

    half = n // 2
    middle = (me >= half - REACH) & (me < half + REACH)
    lacks = jnp.where(me < half, me + REACH, me - REACH)
    place = jnp.where(me < half, 2 * REACH, 0)

    def over(kind, j):
        d = half - REACH + j
        b = d + REACH if j < REACH else d - REACH
        return remote(
            cut(sources[kind], b, width),
            beside_ref.at[2 * REACH if j < REACH else 0, kind, me],
            over_send.at[kind, j],
            over_recv.at[kind, me],
            d,
        )

    def lacking(kind, s):
        return remote(
            cut(sources[kind], lacks, width),
            beside_ref.at[place, kind, s],
            over_send.at[kind, 0],
            over_recv.at[kind, s],
            s,
        )

    def kept(kind):
        return pltpu.make_async_copy(
            cut(sources[kind], lacks, width), beside_ref.at[place, kind, me], over_own.at[kind]
        )

    def arriving(c, d, s):
        return remote(
            across(ens_ref, d, *parts[c]),
            down(x_ref, s, *parts[c]),
            in_send.at[c, d],
            in_recv.at[c, s],
            d,
        )

    def leaving(c, d, s):
        return remote(
            down(stage_ref, d, *pieces[c][:2]),
            across(out_ref, s, *pieces[c][:2]),
            out_send.at[c, d],
            out_recv.at[c, s],
            d,
        )

    def staying(c):
        return pltpu.make_async_copy(
            down(stage_ref, me, *pieces[c][:2]), across(out_ref, me, *pieces[c][:2]), last_sem.at[c]
        )

    def send(first, last):
        for c in range(first, last):

            @pl.loop(1, n)
            def _(i, c=c):
                arriving(c, lax.rem(me + STRIDE * i, n), me).start()

    @pl.loop(1, n)
    def _(i):
        for kind in range(2):
            block(kind, lax.rem(me + STRIDE * i, n), me).start()

    for j in range(2 * REACH):

        @pl.when(me != half - REACH + j)
        def _(j=j):
            for kind in range(2):
                over(kind, j).start()

    @pl.when(middle)
    def _():
        for kind in range(2):
            kept(kind).start()

    send(0, EARLY)

    @pl.loop(1, n)
    def _(i):
        s = lax.rem(me + i, n)
        for kind in range(2):
            block(kind, s, s).wait()

    for copy in own[:2]:
        copy.wait()

    odd = lax.rem(me, 2)
    sibling = me + 1 - 2 * odd
    left = (me >= REACH) & ((me < half) | (me >= half + REACH))
    right = (me < n - REACH) & ((me < half - REACH) | (me >= half))

    def side(src, slot, which, d):
        return remote(beside_ref.at[src], beside_ref.at[slot], side_send.at[which], side_recv.at[slot], d)

    pl.when(right)(lambda: side(REACH, 0, 0, me + 2).start())
    pl.when(left)(lambda: side(REACH, 4, 1, me - 2).start())
    side(REACH, 1 + 2 * odd, 2, sibling).start()
    send(EARLY, len(parts))

    pl.when(right)(lambda: side(REACH, 4, 0, me + 2).wait())
    pl.when(left)(lambda: side(REACH, 0, 1, me - 2).wait())

    for j in range(2 * REACH):

        @pl.when(me != half - REACH + j)
        def _(j=j):
            for kind in range(2):
                over(kind, j).wait_send()

    @pl.when(middle)
    def _():
        for kind in range(2):
            kept(kind).wait()

        @pl.loop(1, n)
        def _(i):
            for kind in range(2):
                lacking(kind, lax.rem(me + i, n)).wait_recv()

    hands = jnp.where(odd == 1, me, n - 1 - me) >= 2
    gets = jnp.where(odd == 1, n - 1 - me, me) >= 2
    hand = side(4 - 4 * odd, 3 - 2 * odd, 3, sibling)
    got = side(4 - 4 * odd, 1 + 2 * odd, 3, sibling)
    pl.when(hands)(lambda: hand.start())

    side(REACH, 3 - 2 * odd, 2, sibling).wait()
    pl.when(hands)(lambda: hand.wait_send())
    pl.when(gets)(lambda: got.wait_recv())

    d_ref, e_in_ref = scratch[:2]
    for i in range(REACHED):
        for b in range(NBD):
            cols = pl.ds(b * CB, CB)
            d_ref[i * NBD + b] = beside_ref[i, 0, :, :, cols].reshape(members, CB)
            e_in_ref[i * NBD + b] = beside_ref[i, 1, :, :, cols].reshape(members, CB)
    for copy in loads:
        copy.wait()
    form_weights(list_ref, count_ref, class_ref, table_ref, obs_ref, noise_ref, wt_ref, *scratch)
    own[2].wait()

    there = -1
    for q, (first, wide, c) in enumerate(pieces):
        if c > there:
            there = c

            @pl.loop(1, n)
            def _(i, c=c):
                s = lax.rem(me + i, n)
                arriving(c, s, s).wait()

        @pl.loop(0, wide // WIDE)
        def _(j, first=first):
            cols = pl.ds(pl.multiple_of(first + j * WIDE, WIDE), WIDE)
            xf = x_ref[:, cols].astype(jnp.float32)
            mean = jnp.sum(xf, axis=0, keepdims=True) * (1.0 / members)
            anomaly = ((xf - mean) * scale).astype(jnp.bfloat16)
            delta = jnp.dot(wt_ref[...], anomaly, preferred_element_type=jnp.float32)
            stage_ref[:, cols] = (xf + delta).astype(jnp.bfloat16)

        @pl.loop(1, n)
        def _(i, q=q):
            leaving(q, lax.rem(me + STRIDE * i, n), me).start()

        staying(q).start()

    for q in range(len(pieces)):

        @pl.loop(1, n)
        def _(i, q=q):
            s = lax.rem(me + i, n)
            leaving(q, s, s).wait()

        staying(q).wait()


def smooth(tables, predicted, perturb, ensemble, n):
    rows, total = ensemble.shape
    members, cells = rows * n, total // n
    outs = sum(len(group) for group in EIGHTHS)
    hbm = pl.BlockSpec(memory_space=pl.ANY)
    sems = pltpu.SemaphoreType.DMA
    return pl.pallas_call(
        functools.partial(smoother_kernel, n),
        out_shape=pltpu.VMEM((rows, total), ensemble.dtype),
        in_specs=[hbm] * 9,
        out_specs=hbm,
        scratch_shapes=[
            *[pltpu.SMEM(t.shape, t.dtype) for t in tables[:4]],
            *[pltpu.VMEM(t.shape, t.dtype) for t in tables[4:]],
            pltpu.VMEM((REACHED, 2, n, rows, predicted.shape[1] // n), jnp.bfloat16),
            pltpu.VMEM((members, cells), jnp.bfloat16),
            pltpu.VMEM((members, cells), jnp.bfloat16),
            pltpu.VMEM((members, members), jnp.bfloat16),
            sems((len(tables),)),
            sems((3,)),
            sems((2, n)),
            sems((2, n)),
            sems((4,)),
            sems((REACHED,)),
            sems((len(EIGHTHS), n)),
            sems((len(EIGHTHS), n)),
            sems((outs, n)),
            sems((outs, n)),
            sems((outs,)),
            sems((2,)),
            sems((2, 2 * REACH)),
            sems((2, n)),
            *weights_scratch(members, tables[0].shape[0]),
        ],
        compiler_params=pltpu.CompilerParams(
            collective_id=1, has_side_effects=True, vmem_limit_bytes=VMEM_MIB * 1024 * 1024
        ),
    )(*tables, predicted, perturb, ensemble)


def solve_weights(tables, beside):
    members = beside.shape[2]
    slots = tables[0].shape[0]
    vmem = pl.BlockSpec(memory_space=pltpu.VMEM)
    smem = pl.BlockSpec(memory_space=pltpu.SMEM)
    return pl.pallas_call(
        weights_kernel,
        out_shape=jax.ShapeDtypeStruct((members, members), jnp.bfloat16),
        in_specs=[smem] * 4 + [vmem] * 3,
        out_specs=vmem,
        scratch_shapes=weights_scratch(members, slots),
        compiler_params=pltpu.CompilerParams(vmem_limit_bytes=32 * 1024 * 1024),
        cost_estimate=pl.CostEstimate(
            flops=60_000_000_000, bytes_accessed=8_000_000, transcendentals=0
        ),
    )(*tables, beside)


def per_device(
    ensemble,
    predicted,
    perturb,
    observed,
    noise_scale,
    block_list,
    block_count,
    taper_class,
    taper_table,
):
    n = lax.axis_size("tile")
    members = ensemble.shape[0] * n
    tables = (
        block_list.T,
        block_count,
        taper_class.T,
        taper_table,
        observed.reshape(-1, CB),
        noise_scale.reshape(-1, CB),
    )
    if ensemble.shape[0] % 16 == 0 and n % 8 == 0:
        return smooth(tables, predicted, perturb, ensemble, n)
    beside = route_blocks(predicted, perturb, n)
    beside, ensemble = lax.optimization_barrier((beside, ensemble))
    tile_x = lax.all_to_all(ensemble, "tile", split_axis=1, concat_axis=0, tiled=True)
    wt = solve_weights(tables, beside)
    xf = tile_x.astype(jnp.float32)
    anomaly = ((xf - jnp.mean(xf, axis=0, keepdims=True)) / jnp.sqrt(members - 1.0)).astype(
        jnp.bfloat16
    )
    delta = lax.dot_general(
        wt, anomaly, (((1,), (0,)), ((), ())), preferred_element_type=jnp.float32
    )
    result = (xf + delta).astype(jnp.bfloat16)
    return lax.all_to_all(result, "tile", split_axis=0, concat_axis=1, tiled=True)


def solution(mesh):
    in_specs = (
        P("tile", "slab"),
        P("tile", "slab"),
        P("tile", "slab"),
        P("slab"),
        P("slab"),
        P(),
        P(),
        P(),
        P(),
    )
    out_specs = P("tile", "slab")
    return jax.shard_map(
        per_device, mesh=mesh, in_specs=in_specs, out_specs=out_specs, check_vma=False
    )
```

```python
import functools
import jax
import jax.numpy as jnp
from jax import lax
from jax.experimental import pallas as pl
from jax.experimental.pallas import tpu as pltpu
from jax.sharding import PartitionSpec as P

CB = 128
REACH = 2
NBD = 2
BLK = 128
PIV = 4

inflation = 4.0
HIGHEST = lax.Precision.HIGHEST
MESH = pl.DeviceIdType.MESH
REACHED = 2 * REACH + 1
WIDE = 1024
EIGHTHS = ((2,), (4, 2))
EARLY = 1
STRIDE = 3
VMEM_MIB = 54


def greet(n, me):
    barrier = pltpu.get_barrier_semaphore()

    @pl.loop(1, n)
    def _(i):
        pl.semaphore_signal(
            barrier, inc=1, device_id={"tile": lax.rem(me + i, n)}, device_id_type=MESH
        )

    pl.semaphore_wait(barrier, n - 1)


def blocks_kernel(n, pred_ref, pert_ref, out_ref, own_sem, send_sem, recv_sem, side_send, side_recv):
    me = lax.axis_index("tile")
    width = out_ref.shape[4]
    sources = (pred_ref, pert_ref)
    mine = out_ref.at[REACH]
    greet(n, me)

    def cut(ref, d):
        return ref.at[:, pl.ds(pl.multiple_of(d * width, CB), width)]

    @pl.loop(0, n - 1)
    def _(i):
        d = lax.rem(me + n // 2 + i, n)
        d = jnp.where(d == me, lax.rem(me + n // 2 + n - 1, n), d)
        for kind, ref in enumerate(sources):
            pltpu.make_async_remote_copy(
                src_ref=cut(ref, d),
                dst_ref=mine.at[kind, me],
                send_sem=send_sem.at[kind, d],
                recv_sem=recv_sem.at[kind, me],
                device_id={"tile": d},
                device_id_type=MESH,
            ).start()

    own = [
        pltpu.make_async_copy(cut(ref, me), mine.at[kind, me], own_sem.at[kind])
        for kind, ref in enumerate(sources)
    ]
    for copy in own:
        copy.start()

    @pl.loop(1, n)
    def _(i):
        s = lax.rem(me + i, n)
        for kind, ref in enumerate(sources):
            pltpu.make_async_remote_copy(
                src_ref=cut(ref, s),
                dst_ref=mine.at[kind, s],
                send_sem=send_sem.at[kind, s],
                recv_sem=recv_sem.at[kind, s],
                device_id={"tile": s},
                device_id_type=MESH,
            ).wait()

    for copy in own:
        copy.wait()

    def beside(offset, slot):
        return pltpu.make_async_remote_copy(
            src_ref=mine,
            dst_ref=out_ref.at[slot],
            send_sem=side_send.at[offset + REACH],
            recv_sem=side_recv.at[slot],
            device_id={"tile": me + offset},
            device_id_type=MESH,
        )

    offsets = [o for r in range(REACH, 0, -1) for o in (r, -r)]
    for offset in offsets:

        @pl.when((me + offset >= 0) & (me + offset < n))
        def _(offset=offset):
            beside(offset, REACH - offset).start()

    for offset in offsets:

        @pl.when((me + offset >= 0) & (me + offset < n))
        def _(offset=offset):
            beside(offset, REACH + offset).wait()


def route_blocks(predicted, perturb, n):
    rows, data = predicted.shape
    hbm = pl.BlockSpec(memory_space=pl.ANY)
    sems = pltpu.SemaphoreType.DMA
    out = pl.pallas_call(
        functools.partial(blocks_kernel, n),
        out_shape=jax.ShapeDtypeStruct((REACHED, 2, n, rows, data // n), predicted.dtype),
        in_specs=[hbm, hbm],
        out_specs=hbm,
        scratch_shapes=[sems((2,)), sems((2, n)), sems((2, n)), sems((REACHED,)), sems((REACHED,))],
        compiler_params=pltpu.CompilerParams(collective_id=0, has_side_effects=True),
        cost_estimate=pl.CostEstimate(
            flops=20_000_000_000, bytes_accessed=8_000_000, transcendentals=0
        ),
    )(predicted, perturb)
    return out.reshape(REACHED, 2, n * rows, data // n)


def invert_block(a_ref):
    n = a_ref.shape[0]
    lane = lax.broadcasted_iota(jnp.int32, (1, n), 1)

    def step(q, carry):
        k0 = q * PIV
        a = a_ref[...]
        cols = [
            jnp.take_along_axis(
                a, jnp.full((n, n), k0 + p, jnp.int32), axis=1, mode="promise_in_bounds"
            )
            for p in range(PIV)
        ]
        rows = [a_ref[pl.ds(k0 + p, 1), :] for p in range(PIV)]
        m = [
            [
                jnp.take_along_axis(
                    jnp.broadcast_to(rows[i], (8, n)),
                    jnp.full((8, n), k0 + j, jnp.int32),
                    axis=1,
                    mode="promise_in_bounds",
                )[0:1]
                for j in range(PIV)
            ]
            for i in range(PIV)
        ]
        for p in range(PIV):
            d = 1.0 / m[p][p]
            new = [[None] * PIV for _ in range(PIV)]
            for j in range(PIV):
                new[p][j] = d if j == p else m[p][j] * d
            for i in range(PIV):
                if i == p:
                    continue
                for j in range(PIV):
                    new[i][j] = -m[i][p] * d if j == p else m[i][j] - m[i][p] * new[p][j]
            m = new
        inside = (lane >= k0) & (lane < k0 + PIV)
        rows = [
            jnp.where(inside, jnp.where(lane == k0 + p, 1.0, 0.0), rows[p]) for p in range(PIV)
        ]
        t = []
        for i in range(PIV):
            acc = m[i][0] * rows[0]
            for j in range(1, PIV):
                acc = acc + m[i][j] * rows[j]
            t.append(acc)
        a = jnp.where(inside, 0.0, a)
        for p in range(PIV):
            a = a - cols[p] * t[p]
        a_ref[...] = a
        for p in range(PIV):
            a_ref[pl.ds(k0 + p, 1), :] = t[p]
        return carry

    lax.fori_loop(0, n // PIV, step, 0)


def form_weights(
    list_ref, count_ref, class_ref, table_ref, obs_ref, noise_ref, wt_ref, d_ref, e_in_ref, z_ref, e_ref, s_ref, a_ref
):
    members = wt_ref.shape[0]
    me = lax.axis_index("tile")
    for k in range(list_ref.shape[0]):
        block = jnp.clip(list_ref[k, me], 0, noise_ref.shape[0] - 1)
        slot = jnp.clip(block - (me - REACH) * NBD, 0, REACHED * NBD - 1)
        level = jnp.clip(class_ref[k, me], 0, table_ref.shape[0] - 1)
        rho = jnp.full((1, CB), table_ref[level], jnp.float32)
        used = jnp.full((1, CB), k, jnp.int32) < jnp.full((1, CB), count_ref[me], jnp.int32)
        weight = jnp.where(used, jnp.sqrt(rho), 0.0)
        noise = noise_ref[pl.ds(block, 1), :]
        zfac = weight / (float((members - 1) * inflation) ** 0.5 * noise)
        cols = pl.ds(k * CB, CB)
        pred = d_ref[slot].astype(jnp.float32)
        pert = e_in_ref[slot].astype(jnp.float32)
        mean = jnp.sum(pred, axis=0, keepdims=True) * (1.0 / members)
        z_ref[:, cols] = ((pred - mean) * zfac).astype(jnp.bfloat16)
        e_ref[:, cols] = (
            ((obs_ref[pl.ds(block, 1), :] - pred) / (float(inflation) ** 0.5 * noise) + pert)
            * weight
        ).astype(jnp.bfloat16)
    dims = (((1,), (1,)), ((), ()))
    eye = (
        lax.broadcasted_iota(jnp.int32, (members, members), 0)
        == lax.broadcasted_iota(jnp.int32, (members, members), 1)
    ).astype(jnp.float32)
    s_ref[:, 0:members] = (
        lax.dot_general(z_ref[...], z_ref[...], dims, preferred_element_type=jnp.float32) + eye
    )
    s_ref[:, members:] = lax.dot_general(
        z_ref[...], e_ref[...], dims, preferred_element_type=jnp.float32
    )
    blocks = members // BLK

    def mm(x, y):
        return jnp.dot(x, y, precision=HIGHEST, preferred_element_type=jnp.float32)

    for k in range(blocks):
        lo, hi = k * BLK, (k + 1) * BLK
        a_ref[...] = s_ref[lo:hi, lo:hi]
        invert_block(a_ref)
        upper = mm(a_ref[...], s_ref[lo:hi, hi:])
        s_ref[lo:hi, hi:] = upper
        if k < blocks - 1:
            s_ref[hi:, hi:] -= mm(s_ref[hi:, lo:hi], upper)
    for k in range(blocks - 2, -1, -1):
        lo, hi = k * BLK, (k + 1) * BLK
        s_ref[lo:hi, members:] -= mm(s_ref[lo:hi, hi:members], s_ref[hi:, members:])
    wt_ref[...] = s_ref[:, members:].T.astype(jnp.bfloat16)


def weights_kernel(
    list_ref, count_ref, class_ref, table_ref, obs_ref, noise_ref, beside_ref, wt_ref, *scratch
):
    d_ref, e_in_ref = scratch[:2]
    for i in range(REACHED):
        for b in range(NBD):
            cols = pl.ds(b * CB, CB)
            d_ref[i * NBD + b] = beside_ref[i, 0, :, cols]
            e_in_ref[i * NBD + b] = beside_ref[i, 1, :, cols]
    form_weights(list_ref, count_ref, class_ref, table_ref, obs_ref, noise_ref, wt_ref, *scratch)


def weights_scratch(members, slots):
    return [
        pltpu.VMEM((REACHED * NBD, members, CB), jnp.bfloat16),
        pltpu.VMEM((REACHED * NBD, members, CB), jnp.bfloat16),
        pltpu.VMEM((members, slots * CB), jnp.bfloat16),
        pltpu.VMEM((members, slots * CB), jnp.bfloat16),
        pltpu.VMEM((members, 2 * members), jnp.float32),
        pltpu.VMEM((BLK, BLK), jnp.float32),
    ]


def smoother_kernel(
    n,
    list_hbm,
    count_hbm,
    class_hbm,
    table_hbm,
    obs_hbm,
    noise_hbm,
    pred_ref,
    pert_ref,
    ens_ref,
    out_ref,
    list_ref,
    count_ref,
    class_ref,
    table_ref,
    obs_ref,
    noise_ref,
    beside_ref,
    x_ref,
    stage_ref,
    wt_ref,
    table_sem,
    own_sem,
    block_send,
    block_recv,
    side_send,
    side_recv,
    in_send,
    in_recv,
    out_send,
    out_recv,
    last_sem,
    over_own,
    over_send,
    over_recv,
    *scratch,
):
    me = lax.axis_index("tile")
    members, cells = x_ref.shape
    rows = members // n
    width = beside_ref.shape[4]
    unit = cells // 8
    parts, pieces = [], []
    for group in EIGHTHS:
        first = sum(w for _, w in parts)
        parts.append((first, sum(group) * unit))
        for w in group:
            pieces.append((first, w * unit, len(parts) - 1))
            first += w * unit
    scale = 1.0 / float(members - 1) ** 0.5
    sources = (pred_ref, pert_ref)
    mine = beside_ref.at[REACH]

    def cut(ref, d, size):
        return ref.at[:, pl.ds(pl.multiple_of(d * size, CB), size)]

    def held(ref, s):
        return ref.at[pl.ds(pl.multiple_of(s * rows, rows), rows), :]

    def across(ref, d, first, wide):
        return ref.at[:, pl.ds(pl.multiple_of(d * cells + first, CB), wide)]

    def down(ref, s, first, wide):
        return ref.at[pl.ds(pl.multiple_of(s * rows, rows), rows), pl.ds(first, wide)]

    small = (
        (list_hbm, list_ref),
        (count_hbm, count_ref),
        (class_hbm, class_ref),
        (table_hbm, table_ref),
        (obs_hbm, obs_ref),
        (noise_hbm, noise_ref),
    )
    loads = [
        pltpu.make_async_copy(src, dst, table_sem.at[i]) for i, (src, dst) in enumerate(small)
    ]
    own = [
        pltpu.make_async_copy(cut(sources[kind], me, width), mine.at[kind, me], own_sem.at[kind])
        for kind in range(2)
    ]
    own.append(pltpu.make_async_copy(cut(ens_ref, me, cells), held(x_ref, me), own_sem.at[2]))
    for copy in own + loads:
        copy.start()
    greet(n, me)

    def remote(src, dst, send, recv, d):
        return pltpu.make_async_remote_copy(
            src_ref=src,
            dst_ref=dst,
            send_sem=send,
            recv_sem=recv,
            device_id={"tile": d},
            device_id_type=MESH,
        )

    def block(kind, d, s):
        return remote(
            cut(sources[kind], d, width),
            mine.at[kind, s],
            block_send.at[kind, d],
            block_recv.at[kind, s],
            d,
        )

    half = n // 2
    middle = (me >= half - REACH) & (me < half + REACH)
    lacks = jnp.where(me < half, me + REACH, me - REACH)
    place = jnp.where(me < half, 2 * REACH, 0)

    def over(kind, j):
        d = half - REACH + j
        b = d + REACH if j < REACH else d - REACH
        return remote(
            cut(sources[kind], b, width),
            beside_ref.at[2 * REACH if j < REACH else 0, kind, me],
            over_send.at[kind, j],
            over_recv.at[kind, me],
            d,
        )

    def lacking(kind, s):
        return remote(
            cut(sources[kind], lacks, width),
            beside_ref.at[place, kind, s],
            over_send.at[kind, 0],
            over_recv.at[kind, s],
            s,
        )

    def kept(kind):
        return pltpu.make_async_copy(
            cut(sources[kind], lacks, width), beside_ref.at[place, kind, me], over_own.at[kind]
        )

    def arriving(c, d, s):
        return remote(
            across(ens_ref, d, *parts[c]),
            down(x_ref, s, *parts[c]),
            in_send.at[c, d],
            in_recv.at[c, s],
            d,
        )

    def leaving(c, d, s):
        return remote(
            down(stage_ref, d, *pieces[c][:2]),
            across(out_ref, s, *pieces[c][:2]),
            out_send.at[c, d],
            out_recv.at[c, s],
            d,
        )

    def staying(c):
        return pltpu.make_async_copy(
            down(stage_ref, me, *pieces[c][:2]), across(out_ref, me, *pieces[c][:2]), last_sem.at[c]
        )

    def send(first, last):
        for c in range(first, last):

            @pl.loop(1, n)
            def _(i, c=c):
                arriving(c, lax.rem(me + STRIDE * i, n), me).start()

    @pl.loop(1, n)
    def _(i):
        for kind in range(2):
            block(kind, lax.rem(me + STRIDE * i, n), me).start()

    for j in range(2 * REACH):

        @pl.when(me != half - REACH + j)
        def _(j=j):
            for kind in range(2):
                over(kind, j).start()

    @pl.when(middle)
    def _():
        for kind in range(2):
            kept(kind).start()

    send(0, EARLY)

    @pl.loop(1, n)
    def _(i):
        s = lax.rem(me + i, n)
        for kind in range(2):
            block(kind, s, s).wait()

    for copy in own[:2]:
        copy.wait()

    odd = lax.rem(me, 2)
    sibling = me + 1 - 2 * odd
    left = (me >= REACH) & ((me < half) | (me >= half + REACH))
    right = (me < n - REACH) & ((me < half - REACH) | (me >= half))

    def side(src, slot, which, d):
        return remote(beside_ref.at[src], beside_ref.at[slot], side_send.at[which], side_recv.at[slot], d)

    pl.when(right)(lambda: side(REACH, 0, 0, me + 2).start())
    pl.when(left)(lambda: side(REACH, 4, 1, me - 2).start())
    side(REACH, 1 + 2 * odd, 2, sibling).start()
    send(EARLY, len(parts))

    pl.when(right)(lambda: side(REACH, 4, 0, me + 2).wait())
    pl.when(left)(lambda: side(REACH, 0, 1, me - 2).wait())

    for j in range(2 * REACH):

        @pl.when(me != half - REACH + j)
        def _(j=j):
            for kind in range(2):
                over(kind, j).wait_send()

    @pl.when(middle)
    def _():
        for kind in range(2):
            kept(kind).wait()

        @pl.loop(1, n)
        def _(i):
            for kind in range(2):
                lacking(kind, lax.rem(me + i, n)).wait_recv()

    hands = jnp.where(odd == 1, me, n - 1 - me) >= 2
    gets = jnp.where(odd == 1, n - 1 - me, me) >= 2
    hand = side(4 - 4 * odd, 3 - 2 * odd, 3, sibling)
    got = side(4 - 4 * odd, 1 + 2 * odd, 3, sibling)
    pl.when(hands)(lambda: hand.start())

    side(REACH, 3 - 2 * odd, 2, sibling).wait()
    pl.when(hands)(lambda: hand.wait_send())
    pl.when(gets)(lambda: got.wait_recv())

    d_ref, e_in_ref = scratch[:2]
    for i in range(REACHED):
        for b in range(NBD):
            cols = pl.ds(b * CB, CB)
            d_ref[i * NBD + b] = beside_ref[i, 0, :, :, cols].reshape(members, CB)
            e_in_ref[i * NBD + b] = beside_ref[i, 1, :, :, cols].reshape(members, CB)
    for copy in loads:
        copy.wait()
    form_weights(list_ref, count_ref, class_ref, table_ref, obs_ref, noise_ref, wt_ref, *scratch)
    own[2].wait()

    there = -1
    for q, (first, wide, c) in enumerate(pieces):
        if c > there:
            there = c

            @pl.loop(1, n)
            def _(i, c=c):
                s = lax.rem(me + i, n)
                arriving(c, s, s).wait()

        @pl.loop(0, wide // WIDE)
        def _(j, first=first):
            cols = pl.ds(pl.multiple_of(first + j * WIDE, WIDE), WIDE)
            xf = x_ref[:, cols].astype(jnp.float32)
            mean = jnp.sum(xf, axis=0, keepdims=True) * (1.0 / members)
            anomaly = ((xf - mean) * scale).astype(jnp.bfloat16)
            delta = jnp.dot(wt_ref[...], anomaly, preferred_element_type=jnp.float32)
            stage_ref[:, cols] = (xf + delta).astype(jnp.bfloat16)

        @pl.loop(1, n)
        def _(i, q=q):
            leaving(q, lax.rem(me + STRIDE * i, n), me).start()

        staying(q).start()

    for q in range(len(pieces)):

        @pl.loop(1, n)
        def _(i, q=q):
            s = lax.rem(me + i, n)
            leaving(q, s, s).wait()

        staying(q).wait()


def smooth(tables, predicted, perturb, ensemble, n):
    rows, total = ensemble.shape
    members, cells = rows * n, total // n
    outs = sum(len(group) for group in EIGHTHS)
    hbm = pl.BlockSpec(memory_space=pl.ANY)
    sems = pltpu.SemaphoreType.DMA
    return pl.pallas_call(
        functools.partial(smoother_kernel, n),
        out_shape=pltpu.VMEM((rows, total), ensemble.dtype),
        in_specs=[hbm] * 9,
        out_specs=hbm,
        scratch_shapes=[
            *[pltpu.SMEM(t.shape, t.dtype) for t in tables[:4]],
            *[pltpu.VMEM(t.shape, t.dtype) for t in tables[4:]],
            pltpu.VMEM((REACHED, 2, n, rows, predicted.shape[1] // n), jnp.bfloat16),
            pltpu.VMEM((members, cells), jnp.bfloat16),
            pltpu.VMEM((members, cells), jnp.bfloat16),
            pltpu.VMEM((members, members), jnp.bfloat16),
            sems((len(tables),)),
            sems((3,)),
            sems((2, n)),
            sems((2, n)),
            sems((4,)),
            sems((REACHED,)),
            sems((len(EIGHTHS), n)),
            sems((len(EIGHTHS), n)),
            sems((outs, n)),
            sems((outs, n)),
            sems((outs,)),
            sems((2,)),
            sems((2, 2 * REACH)),
            sems((2, n)),
            *weights_scratch(members, tables[0].shape[0]),
        ],
        compiler_params=pltpu.CompilerParams(
            collective_id=1, has_side_effects=True, vmem_limit_bytes=VMEM_MIB * 1024 * 1024
        ),
    )(*tables, predicted, perturb, ensemble)


def solve_weights(tables, beside):
    members = beside.shape[2]
    slots = tables[0].shape[0]
    vmem = pl.BlockSpec(memory_space=pltpu.VMEM)
    smem = pl.BlockSpec(memory_space=pltpu.SMEM)
    return pl.pallas_call(
        weights_kernel,
        out_shape=jax.ShapeDtypeStruct((members, members), jnp.bfloat16),
        in_specs=[smem] * 4 + [vmem] * 3,
        out_specs=vmem,
        scratch_shapes=weights_scratch(members, slots),
        compiler_params=pltpu.CompilerParams(vmem_limit_bytes=32 * 1024 * 1024),
        cost_estimate=pl.CostEstimate(
            flops=60_000_000_000, bytes_accessed=8_000_000, transcendentals=0
        ),
    )(*tables, beside)


def per_device(
    ensemble,
    predicted,
    perturb,
    observed,
    noise_scale,
    block_list,
    block_count,
    taper_class,
    taper_table,
):
    n = lax.axis_size("tile")
    members = ensemble.shape[0] * n
    tables = (
        block_list.T,
        block_count,
        taper_class.T,
        taper_table,
        observed.reshape(-1, CB),
        noise_scale.reshape(-1, CB),
    )
    if ensemble.shape[0] % 16 == 0 and n % 8 == 0:
        return smooth(tables, predicted, perturb, ensemble, n)
    beside = route_blocks(predicted, perturb, n)
    beside, ensemble = lax.optimization_barrier((beside, ensemble))
    tile_x = lax.all_to_all(ensemble, "tile", split_axis=1, concat_axis=0, tiled=True)
    wt = solve_weights(tables, beside)
    xf = tile_x.astype(jnp.float32)
    anomaly = ((xf - jnp.mean(xf, axis=0, keepdims=True)) / jnp.sqrt(members - 1.0)).astype(
        jnp.bfloat16
    )
    delta = lax.dot_general(
        wt, anomaly, (((1,), (0,)), ((), ())), preferred_element_type=jnp.float32
    )
    result = (xf + delta).astype(jnp.bfloat16)
    return lax.all_to_all(result, "tile", split_axis=0, concat_axis=1, tiled=True)


def solution(mesh):
    in_specs = (
        P("tile", "slab"),
        P("tile", "slab"),
        P("tile", "slab"),
        P("slab"),
        P("slab"),
        P(),
        P(),
        P(),
        P(),
    )
    out_specs = P("tile", "slab")
    return jax.shard_map(
        per_device, mesh=mesh, in_specs=in_specs, out_specs=out_specs, check_vma=False
    )
```
